128 devices in a mesh: shot: 2 (over core), gx: 8 (over y_lo, x), gy: 8 (over z, y_hi).
Axes of the slice: x: 4, y: 4 (y_hi: 2, y_lo: 2; y = y_hi * 2 + y_lo), z: 4, core: 2. Of those that a mesh axis runs over, the one named last changes fastest.
Arguments:
- adjoint_prev: float32 [2, 256, 256, 512], P('shot', 'gx', 'gy'), may hold values from -6 to 6
- adjoint_now: float32 [2, 256, 256, 512], P('shot', 'gx', 'gy'), may hold values from -6 to 6
- speed_term: float32 [2, 256, 256, 512], P('shot', 'gx', 'gy'), may hold values from 0.05 to 0.25
- adjoint_source: float32 [2, 2, 256, 256, 512], P('shot', None, 'gx', 'gy'), may hold values from -6 to 6
- forward_accel: float32 [2, 2, 256, 256, 512], P('shot', None, 'gx', 'gy'), may hold values from -6 to 6
- footprint: int32 [2, 8, 8, 512], P('shot', 'gx', 'gy'), may hold values from 0 to 16383, as said below
- live_counts: int32 [2, 8, 8], P('shot', 'gx', 'gy'), may hold values from 256 to 512, as said below
Outputs:
- level_one: float32 [2, 256, 256, 512], P('shot', 'gx', 'gy')
- level_two: float32 [2, 256, 256, 512], P('shot', 'gx', 'gy')
- model_gradient: float32 [16384, 1024], P(('shot', 'gx', 'gy'))
The draws below stay inside these ranges and needn't reach their ends.
Inputs may be any that keep to these rules, and one draw needn't show every extreme that they name: `footprint`: among the 512 entries of one device's list, each owner device o (entries with id // 128 == o, owners numbered over shot, gx, gy in that order) appears exactly 4 times; live and dead entries alike. Entries at positions from live_counts on are dead and contribute nothing.
All inputs are finite; a program needn't handle non-finite values.
Results may differ from the reference program's by a relative error of at most 0.0029.
Values may be sent and summed in bfloat16 or wider, within the bound.
No kernel may reach another device: no remote copies, remote signals or barrier semaphores. Data moves between devices by JAX's collectives and lax.ppermute only.
A program may use at most 128 MiB of HBM per device.

```python
import jax
import jax.numpy as jnp

CX = 32
CY = 32
CZ = 512
TX = 8
TY = 8
TZ = 16
GROUPS = 2
NX = 256
NY = 256
TILE = 1024
SUB = 512
OWNERS = 128
CAP = 4
TILES_DEV = 128
NTILES = 16384
N_GX = 8
N_GY = 8


def draw_footprint(key, part):
    row_count = GROUPS * (NX // CX) * (NY // CY)
    keys = jax.random.split(jax.random.fold_in(key, 11), row_count)
    shuffled = jax.vmap(lambda single: jax.random.permutation(single, OWNERS))(keys)
    owner_ids = jnp.repeat(shuffled, CAP, axis=1)
    slot_ids = jax.random.randint(jax.random.fold_in(key, 12), (row_count, SUB), 0, TILES_DEV)
    listed = owner_ids * TILES_DEV + slot_ids
    return listed.reshape(GROUPS, NX // CX, NY // CY, SUB).astype(jnp.int32)


def draw_live_counts(key, part):
    row_count = GROUPS * (NX // CX) * (NY // CY)
    values = jax.random.randint(jax.random.fold_in(key, 21), (row_count,), SUB // 2, SUB + 1)
    chosen = jax.random.randint(jax.random.fold_in(key, 22), (), 0, row_count)
    values = jnp.where(jnp.arange(row_count) == chosen, SUB, values)
    return values.reshape(GROUPS, NX // CX, NY // CY).astype(jnp.int32)


def steps_of(stream_key, extent, pieces, least, high):
    level = 1.0
    for position, parts in pieces:
        steps = jax.random.uniform(jax.random.fold_in(jax.random.fold_in(stream_key, 6), position), (parts,), jnp.float32, least / len(pieces), high / len(pieces))
        level = level * jnp.repeat(jnp.exp(steps), extent[position] // parts).reshape((-1,) + (1,) * (len(extent) - 1 - position))
    return level


def noise(stream_key, dims, deviation, most, cuts=(), held_as=jnp.bfloat16):
    factor_of = steps_of(stream_key, dims, cuts, -0.22, 0.18) if cuts else 1.0
    entries = jax.random.normal(stream_key, dims, jnp.float32) * deviation * factor_of
    return jnp.minimum(jnp.maximum(entries, -most), most).astype(held_as)


def setup_inputs(seed: int = 0) -> dict:
    streams_of = jax.random.split(jax.random.key(seed), 8)
    adjoint_prev = noise(streams_of[0], (GROUPS, NX, NY, CZ), 1.0, 6.0, ((0, 2), (1, 8), (2, 8)), jnp.float32)
    adjoint_now = noise(streams_of[1], (GROUPS, NX, NY, CZ), 1.0, 6.0, ((0, 2), (1, 8), (2, 8)), jnp.float32)
    speed_term = jnp.clip(0.05 + 0.2 * jax.random.uniform(streams_of[2], (GROUPS, NX, NY, CZ), jnp.float32) ** steps_of(streams_of[2], (GROUPS, NX, NY, CZ), ((0, 2), (1, 8), (2, 8)), -0.2, 0.2), 0.05, 0.25)
    adjoint_source = noise(streams_of[3], (GROUPS, 2, NX, NY, CZ), 1.0, 6.0, ((0, 2), (2, 8), (3, 8)), jnp.float32)
    forward_accel = noise(streams_of[4], (GROUPS, 2, NX, NY, CZ), 1.0, 6.0, ((0, 2), (2, 8), (3, 8)), jnp.float32)
    footprint = draw_footprint(jax.random.fold_in(streams_of[7], 71), 0)
    live_counts = draw_live_counts(jax.random.fold_in(streams_of[7], 71), 0)
    return dict(adjoint_prev=adjoint_prev, adjoint_now=adjoint_now, speed_term=speed_term, adjoint_source=adjoint_source, forward_accel=forward_accel, footprint=footprint, live_counts=live_counts)


CENTER = -205.0 / 72.0
COEFFS = (8.0 / 5.0, -1.0 / 5.0, 8.0 / 315.0, -1.0 / 560.0)


def laplace(values):
    cells_wide, cells_long, cells_deep = values.shape
    padded = jnp.pad(values, 4)

    def window(first_shift, second_shift, third_shift):
        return padded[4 + first_shift:4 + first_shift + cells_wide, 4 + second_shift:4 + second_shift + cells_long, 4 + third_shift:4 + third_shift + cells_deep]

    summed = (3.0 * CENTER) * values
    for offset, weight in enumerate(COEFFS, 1):
        nearby = window(offset, 0, 0) + window(-offset, 0, 0)
        nearby = nearby + window(0, offset, 0) + window(0, -offset, 0)
        nearby = nearby + window(0, 0, offset) + window(0, 0, -offset)
        summed = summed + weight * nearby
    return summed


def advance(earlier, current, velocity, source):
    return 2.0 * current - earlier + velocity * laplace(current) + source


def reference(adjoint_prev, adjoint_now, speed_term, adjoint_source, forward_accel, footprint, live_counts):
    tiles_wide = CX // TX
    tiles_long = CY // TY
    tiles_deep = CZ // TZ
    summed = jnp.zeros((NTILES + 1, TILE), jnp.float32)
    firsts = []
    seconds = []
    for member in range(GROUPS):
        stepped_one = advance(adjoint_prev[member], adjoint_now[member], speed_term[member], adjoint_source[member, 0])
        stepped_two = advance(adjoint_now[member], stepped_one, speed_term[member], adjoint_source[member, 1])
        imaging = forward_accel[member, 0] * stepped_one + forward_accel[member, 1] * stepped_two
        blocks = imaging.reshape(N_GX, tiles_wide, TX, N_GY, tiles_long, TY, tiles_deep, TZ)
        blocks = blocks.transpose(0, 3, 1, 4, 6, 2, 5, 7).reshape(N_GX, N_GY, SUB, TILE).astype(jnp.bfloat16)
        active = jnp.arange(SUB, dtype=jnp.int32)[None, None, :] < live_counts[member][:, :, None]
        target = jnp.where(active, footprint[member], NTILES).reshape(-1).astype(jnp.int32)
        summed = summed.at[target].add(blocks.reshape(-1, TILE).astype(jnp.float32))
        firsts.append(stepped_one)
        seconds.append(stepped_two)
    return (jnp.stack(firsts), jnp.stack(seconds), summed[:NTILES])
```

```python
import jax
import jax.numpy as jnp
from jax import lax
from jax.experimental import pallas as pl
from jax.experimental.pallas import tpu as pltpu
from jax.sharding import PartitionSpec as P

CENTER = -205.0 / 72.0
COEFFS = (8.0 / 5.0, -1.0 / 5.0, 8.0 / 315.0, -1.0 / 560.0)

CX = 32
CY = 32
CZ = 512
XB = 8
OWNERS = 128
CAP = 4
SLABS = 9
NDEV = 8

F32 = jnp.float32
BF16 = jnp.bfloat16
VMEM_LIMIT = 60 * 1024 * 1024

SWAP_A = [(i, i ^ 1) for i in range(NDEV)]
SWAP_B = [(i, (i + 1) % NDEV if i % 2 else (i - 1) % NDEV) for i in range(NDEV)]


def swap_faces(x0, x1, y0, y1):
    return (
        lax.ppermute(x0, "gx", SWAP_A),
        lax.ppermute(x1, "gx", SWAP_B),
        lax.ppermute(y0, "gy", SWAP_A),
        lax.ppermute(y1, "gy", SWAP_B),
    )


def place_halos(ext, rx0, rx1, ry0, ry1, gx, gy):
    def put_x(low, high):
        ext[0:4, 8:40, :] = low[...].astype(F32)
        ext[36:40, 8:40, :] = high[...].astype(F32)

    def put_y(low, high):
        ext[4:36, 4:8, :] = low[...].astype(F32)
        ext[4:36, 40:44, :] = high[...].astype(F32)

    @pl.when(gx % 2 == 1)
    def _():
        put_x(rx0, rx1)

    @pl.when(gx % 2 == 0)
    def _():
        put_x(rx1, rx0)

    @pl.when(gy % 2 == 1)
    def _():
        put_y(ry0, ry1)

    @pl.when(gy % 2 == 0)
    def _():
        put_y(ry1, ry0)

    @pl.when(gx == 0)
    def _():
        ext[0:4, 8:40, :] = jnp.zeros((4, CY, CZ), F32)

    @pl.when(gx == NDEV - 1)
    def _():
        ext[36:40, 8:40, :] = jnp.zeros((4, CY, CZ), F32)

    @pl.when(gy == 0)
    def _():
        ext[4:36, 4:8, :] = jnp.zeros((CX, 4, CZ), F32)

    @pl.when(gy == NDEV - 1)
    def _():
        ext[4:36, 40:44, :] = jnp.zeros((CX, 4, CZ), F32)


def laplace_rows(ext, x, ty):
    rows = ext[x + 4, 8 * ty : 8 * ty + 24, :]
    middle = rows[8:16]
    lane = lax.broadcasted_iota(jnp.int32, (8, CZ), 1)
    summed = (3.0 * CENTER) * middle
    for k, weight in enumerate(COEFFS, 1):
        nearby = ext[x + 4 + k, 8 * ty + 8 : 8 * ty + 16, :] + ext[x + 4 - k, 8 * ty + 8 : 8 * ty + 16, :]
        nearby = nearby + rows[8 + k : 16 + k] + rows[8 - k : 16 - k]
        nearby = nearby + jnp.where(lane >= k, pltpu.roll(middle, k, 1), 0.0)
        nearby = nearby + jnp.where(lane < CZ - k, pltpu.roll(middle, CZ - k, 1), 0.0)
        summed = summed + weight * nearby
    return summed, middle


def first_kernel(
    where_ref, now_hbm, rx0, rx1, ry0, ry1, prev_ref, speed_ref, source_ref,
    one_ref, sx0, sx1, sy0, sy1, ext, sem,
):
    step = pl.program_id(0)
    gx = where_ref[0]
    gy = where_ref[1]

    @pl.when(step == 0)
    def _():
        copy = pltpu.make_async_copy(now_hbm.at[0], ext.at[4:36, 8:40, :], sem)
        copy.start()
        place_halos(ext, rx0, rx1, ry0, ry1, gx, gy)
        copy.wait()

    def plane(xl, carry):
        x = step * XB + xl
        for ty in range(4):
            rows = slice(8 * ty, 8 * ty + 8)
            summed, middle = laplace_rows(ext, x, ty)
            one_ref[0, xl, rows, :] = (
                2.0 * middle - prev_ref[0, xl, rows, :] + speed_ref[0, xl, rows, :] * summed
                + source_ref[0, 0, xl, rows, :]
            )
        return carry

    lax.fori_loop(0, XB, plane, 0)

    @pl.when((step == 0) & (gx % 2 == 1))
    def _():
        sx0[...] = one_ref[0, 0:4].astype(BF16)

    @pl.when((step == 0) & (gx % 2 == 0))
    def _():
        sx1[...] = one_ref[0, 0:4].astype(BF16)

    @pl.when((step == 3) & (gx % 2 == 1))
    def _():
        sx1[...] = one_ref[0, 4:8].astype(BF16)

    @pl.when((step == 3) & (gx % 2 == 0))
    def _():
        sx0[...] = one_ref[0, 4:8].astype(BF16)

    @pl.when(gy % 2 == 1)
    def _():
        sy0[...] = one_ref[0, :, 0:4, :].astype(BF16)
        sy1[...] = one_ref[0, :, 28:32, :].astype(BF16)

    @pl.when(gy % 2 == 0)
    def _():
        sy1[...] = one_ref[0, :, 0:4, :].astype(BF16)
        sy0[...] = one_ref[0, :, 28:32, :].astype(BF16)


def swap_granules(vals):
    granule = lax.broadcasted_iota(jnp.int32, (8, 128), 1) // 16
    vals = list(vals)
    for bit in (1, 2, 4):
        mask = (granule & bit) != 0
        for i in range(8):
            if i & bit:
                continue
            low, high = vals[i], vals[i + bit]
            vals[i] = jnp.where(mask, pltpu.roll(high, 16 * bit, 1), low)
            vals[i + bit] = jnp.where(mask, high, pltpu.roll(low, 128 - 16 * bit, 1))
    return vals


def second_kernel(
    where_ref, foot_ref, live_ref, one_hbm, rx0, rx1, ry0, ry1, now_ref, speed_ref, source_ref, forward_ref,
    two_ref, out_ref, ext, image, slots, count, sem,
):
    step = pl.program_id(0)
    gx = where_ref[0]
    gy = where_ref[1]

    @pl.when(step == 0)
    def _():
        copy = pltpu.make_async_copy(one_hbm.at[0], ext.at[4:36, 8:40, :], sem)
        copy.start()
        for o in range(OWNERS):
            count[o] = 0
        place_halos(ext, rx0, rx1, ry0, ry1, gx, gy)
        copy.wait()

    for ty in range(4):
        rows = slice(8 * ty, 8 * ty + 8)

        def plane(xl, carry):
            x = step * XB + xl
            summed, middle = laplace_rows(ext, x, ty)
            two = (
                2.0 * middle - now_ref[0, xl, rows, :] + speed_ref[0, xl, rows, :] * summed
                + source_ref[0, 0, xl, rows, :]
            )
            two_ref[0, xl, rows, :] = two
            image[xl] = forward_ref[0, 0, xl, rows, :] * middle + forward_ref[0, 1, xl, rows, :] * two
            return carry

        lax.fori_loop(0, XB, plane, 0)

        for zv in range(4):
            pieces = swap_granules([image[x, :, 128 * zv : 128 * zv + 128] for x in range(XB)])
            for p in range(8):
                s = step * 128 + ty * 32 + zv * 8 + p
                listed = foot_ref[s]
                owner = listed // OWNERS
                rank = count[owner]
                count[owner] = rank + 1
                at = owner * SLABS + 2 * rank
                piece = pieces[p].astype(BF16)
                out_ref[at] = piece[0:4]
                out_ref[at + 1] = piece[4:8]
                slot = jnp.where(s < live_ref[0], listed % OWNERS, -1).astype(F32)
                slots[owner, pl.ds(rank, 1), :] = jnp.full((1, 128), slot, F32)

    @pl.when(step == 3)
    def _():
        def put(o, carry):
            out_ref[o * SLABS + 8] = slots[o].astype(BF16)
            return carry

        lax.fori_loop(0, OWNERS, put, 0)


def owner_kernel(in_ref, grad_ref, rows, ids, spread):
    def unpack(j, carry):
        halves = []
        for b in range(2):
            source = 2 * j + b
            for k in range(CAP):
                rows[source * CAP + k, 0:4, :] = in_ref[source * SLABS + 2 * k].astype(F32)
                rows[source * CAP + k, 4:8, :] = in_ref[source * SLABS + 2 * k + 1].astype(F32)
            halves.append(in_ref[source * SLABS + 8].astype(F32))
        ids[pl.ds(8 * j, 8), :] = jnp.concatenate(halves, axis=0)
        return carry

    lax.fori_loop(0, OWNERS // 2, unpack, 0)
    slot = lax.broadcasted_iota(jnp.int32, (OWNERS * CAP, 128), 1).astype(F32)
    onehot = jnp.where(ids[...] == slot, 1.0, 0.0).astype(BF16)
    for y in range(8):
        spread[:, 128 * y : 128 * y + 128] = lax.dot_general(
            onehot, rows[:, y, :].astype(BF16), (((0,), (0,)), ((), ())), preferred_element_type=F32
        )
    for t in range(16):
        at = slice(8 * t, 8 * t + 8)
        vals = swap_granules([spread[at, 128 * y : 128 * y + 128] for y in range(8)])
        for x in range(8):
            grad_ref[at, 128 * x : 128 * x + 128] = vals[x]


def whole(shape):
    return pl.BlockSpec(shape, lambda i: (0,) * len(shape))


SMEM = pl.BlockSpec(memory_space=pltpu.SMEM)
HBM = pl.BlockSpec(memory_space=pl.ANY)
PLANES = pl.BlockSpec((1, XB, CY, CZ), lambda i: (0, i, 0, 0))
FACE_X = whole((4, CY, CZ))
FACE_Y = whole((CX, 4, CZ))
PARAMS = pltpu.CompilerParams(dimension_semantics=("arbitrary",), vmem_limit_bytes=VMEM_LIMIT)


def picked(half):
    return pl.BlockSpec((1, 1, XB, CY, CZ), lambda i: (0, half, i, 0, 0))


def per_device(
    adjoint_prev, adjoint_now, speed_term, adjoint_source, forward_accel, footprint, live_counts
):
    gx = lax.axis_index("gx").astype(jnp.int32)
    gy = lax.axis_index("gy").astype(jnp.int32)
    place = jnp.stack([gx, gy])
    current = adjoint_now[0]
    odd_x = gx % 2 == 1
    odd_y = gy % 2 == 1
    x_low, x_high = current[0:4].astype(BF16), current[28:32].astype(BF16)
    y_low, y_high = current[:, 0:4].astype(BF16), current[:, 28:32].astype(BF16)
    faces = swap_faces(
        jnp.where(odd_x, x_low, x_high),
        jnp.where(odd_x, x_high, x_low),
        jnp.where(odd_y, y_low, y_high),
        jnp.where(odd_y, y_high, y_low),
    )
    face_x = jax.ShapeDtypeStruct((4, CY, CZ), BF16)
    face_y = jax.ShapeDtypeStruct((CX, 4, CZ), BF16)
    face_y_planes = pl.BlockSpec((XB, 4, CZ), lambda i: (i, 0, 0))
    level = jax.ShapeDtypeStruct((1, CX, CY, CZ), F32)
    level_one, *send = pl.pallas_call(
        first_kernel,
        grid=(CX // XB,),
        in_specs=[SMEM, HBM, FACE_X, FACE_X, FACE_Y, FACE_Y, PLANES, PLANES, picked(0)],
        out_specs=[PLANES, FACE_X, FACE_X, face_y_planes, face_y_planes],
        out_shape=[level, face_x, face_x, face_y, face_y],
        scratch_shapes=[pltpu.VMEM((CX + 8, CY + 16, CZ), F32), pltpu.SemaphoreType.DMA],
        compiler_params=PARAMS,
        name="level_one",
    )(place, adjoint_now, *faces, adjoint_prev, speed_term, adjoint_source)
    faces = swap_faces(*send)
    level_two, outgoing = pl.pallas_call(
        second_kernel,
        grid=(CX // XB,),
        in_specs=[
            SMEM, SMEM, SMEM, HBM, FACE_X, FACE_X, FACE_Y, FACE_Y, PLANES, PLANES, picked(1),
            pl.BlockSpec((1, 2, XB, CY, CZ), lambda i: (0, 0, i, 0, 0)),
        ],
        out_specs=[PLANES, whole((OWNERS * SLABS, 4, 128))],
        out_shape=[level, jax.ShapeDtypeStruct((OWNERS * SLABS, 4, 128), BF16)],
        scratch_shapes=[
            pltpu.VMEM((CX + 8, CY + 16, CZ), F32),
            pltpu.VMEM((XB, 8, CZ), F32),
            pltpu.VMEM((OWNERS, CAP, 128), F32),
            pltpu.SMEM((OWNERS,), jnp.int32),
            pltpu.SemaphoreType.DMA,
        ],
        compiler_params=PARAMS,
        name="level_two",
    )(
        place, footprint.reshape(-1), live_counts.reshape(-1), level_one, *faces,
        adjoint_now, speed_term, adjoint_source, forward_accel,
    )
    incoming = lax.all_to_all(outgoing, ("shot", "gx", "gy"), split_axis=0, concat_axis=0, tiled=True)
    gradient = pl.pallas_call(
        owner_kernel,
        out_shape=jax.ShapeDtypeStruct((OWNERS, 1024), F32),
        scratch_shapes=[
            pltpu.VMEM((OWNERS * CAP, 8, 128), F32),
            pltpu.VMEM((OWNERS * CAP, 128), F32),
            pltpu.VMEM((OWNERS, 1024), F32),
        ],
        compiler_params=pltpu.CompilerParams(vmem_limit_bytes=VMEM_LIMIT),
        name="owner_sum",
    )(incoming)
    return (level_one, level_two, gradient)


def solution(mesh):
    return jax.shard_map(
        per_device,
        mesh=mesh,
        in_specs=(
            P("shot", "gx", "gy", None),
            P("shot", "gx", "gy", None),
            P("shot", "gx", "gy", None),
            P("shot", None, "gx", "gy", None),
            P("shot", None, "gx", "gy", None),
            P("shot", "gx", "gy", None),
            P("shot", "gx", "gy"),
        ),
        out_specs=(
            P("shot", "gx", "gy", None),
            P("shot", "gx", "gy", None),
            P(("shot", "gx", "gy"), None),
        ),
        check_vma=False,
    )
```

```python
import jax
import jax.numpy as jnp
import numpy as np
from jax import lax
from jax.experimental import pallas as pl
from jax.experimental.pallas import tpu as pltpu
from jax.sharding import PartitionSpec as P

CENTER = -205.0 / 72.0
COEFFS = (8.0 / 5.0, -1.0 / 5.0, 8.0 / 315.0, -1.0 / 560.0)

CX = 32
CY = 32
CZ = 512
OWNERS = 128
CAP = 4
SUB = 512
SLABS = 9
NDEV = 8

F32 = jnp.float32
BF16 = jnp.bfloat16
MIB = 1024 * 1024

SWAP_A = [(i, i ^ 1) for i in range(NDEV)]
SWAP_B = [(i, (i + 1) % NDEV if i % 2 else (i - 1) % NDEV) for i in range(NDEV)]


def depth_band():
    band = np.zeros((CZ, CZ), np.float64)
    for k, weight in enumerate(COEFFS, 1):
        band += weight * (np.eye(CZ, k=k) + np.eye(CZ, k=-k))
    high = band.astype(jnp.bfloat16)
    low = (band - high.astype(np.float64)).astype(jnp.bfloat16)
    return high, low


def swap_faces(x0, x1, y0, y1):
    return (
        lax.ppermute(x0, "gx", SWAP_A),
        lax.ppermute(x1, "gx", SWAP_B),
        lax.ppermute(y0, "gy", SWAP_A),
        lax.ppermute(y1, "gy", SWAP_B),
    )


def emit_faces(get_x, get_y, gx, gy, sx0, sx1, sy0, sy1):
    @pl.when(gx % 2 == 1)
    def _():
        sx0[...] = get_x(0).astype(BF16)
        sx1[...] = get_x(1).astype(BF16)

    @pl.when(gx % 2 == 0)
    def _():
        sx0[...] = get_x(1).astype(BF16)
        sx1[...] = get_x(0).astype(BF16)

    @pl.when(gy % 2 == 1)
    def _():
        sy0[...] = get_y(0).astype(BF16)
        sy1[...] = get_y(1).astype(BF16)

    @pl.when(gy % 2 == 0)
    def _():
        sy0[...] = get_y(1).astype(BF16)
        sy1[...] = get_y(0).astype(BF16)


def face_kernel(where_ref, now_hbm, sx0, sx1, sy0, sy1, xs, ys, sems):
    gx = where_ref[0]
    gy = where_ref[1]
    copies = [
        pltpu.make_async_copy(now_hbm.at[0, 0:4], xs.at[0], sems.at[0]),
        pltpu.make_async_copy(now_hbm.at[0, 28:32], xs.at[1], sems.at[1]),
        pltpu.make_async_copy(now_hbm.at[0, :, 0:8, :], ys.at[0], sems.at[2]),
        pltpu.make_async_copy(now_hbm.at[0, :, 24:32, :], ys.at[1], sems.at[3]),
    ]
    for copy in copies:
        copy.start()
    for copy in copies:
        copy.wait()
    emit_faces(
        lambda side: xs[side], lambda side: ys[side, :, 4 * side : 4 * side + 4, :], gx, gy, sx0, sx1, sy0, sy1
    )


def depth_terms(values, high_ref, low_ref, zs):
    for i in range(4):
        block = values[0, 8 * i : 8 * i + 8].reshape(8 * CY, CZ)
        big = block.astype(BF16)
        small = (block - big.astype(F32)).astype(BF16)
        term = jnp.dot(big, high_ref[...], preferred_element_type=F32)
        term = term + jnp.dot(big, low_ref[...], preferred_element_type=F32)
        term = term + jnp.dot(small, high_ref[...], preferred_element_type=F32)
        zs[8 * i : 8 * i + 8] = term.reshape(8, CY, CZ)


def extend(values, ext):
    ext[0:4, 8:40, :] = jnp.zeros((4, CY, CZ), F32)
    ext[36:40, 8:40, :] = jnp.zeros((4, CY, CZ), F32)

    def fill(x, carry):
        ext[x + 4, 0:8, :] = jnp.zeros((8, CZ), F32)
        ext[x + 4, 8:40, :] = values[0, x]
        ext[x + 4, 40:48, :] = jnp.zeros((8, CZ), F32)
        return carry

    lax.fori_loop(0, CX, fill, 0)


def laplace_rows(ext, zs, x, ty):
    rows = ext[x + 4, 8 * ty : 8 * ty + 24, :]
    middle = rows[8:16]
    summed = (3.0 * CENTER) * middle + zs[x, 8 * ty : 8 * ty + 8, :]
    for k, weight in enumerate(COEFFS, 1):
        nearby = ext[x + 4 + k, 8 * ty + 8 : 8 * ty + 16, :] + ext[x + 4 - k, 8 * ty + 8 : 8 * ty + 16, :]
        nearby = nearby + rows[8 + k : 16 + k] + rows[8 - k : 16 - k]
        summed = summed + weight * nearby
    return summed, middle


def first_kernel(
    foot_ref, live_ref, now_ref, prev_ref, speed_ref, source_ref, high_ref, low_ref,
    one_ref, out_ref, at_ref, ext, zs, slots, count,
):
    for o in range(OWNERS):
        count[o] = 0
    depth_terms(now_ref, high_ref, low_ref, zs)
    extend(now_ref, ext)
    live = live_ref[0]

    def plane(x, carry):
        for j in range(SUB // CX):
            s = x * (SUB // CX) + j
            listed = foot_ref[s]
            owner = listed // OWNERS
            rank = count[owner]
            count[owner] = rank + 1
            at_ref[s] = owner * SLABS + 2 * rank
            slot = jnp.where(s < live, listed % OWNERS, -1).astype(F32)
            slots[owner, pl.ds(rank, 1), :] = jnp.full((1, 128), slot, F32)
        for ty in range(4):
            rows = slice(8 * ty, 8 * ty + 8)
            summed, middle = laplace_rows(ext, zs, x, ty)
            one_ref[0, x, rows, :] = (
                2.0 * middle - prev_ref[0, x, rows, :] + speed_ref[0, x, rows, :] * summed
                + source_ref[0, 0, x, rows, :]
            )
        return carry

    lax.fori_loop(0, CX, plane, 0)

    def put(o, carry):
        out_ref[o * SLABS + 8] = slots[o].astype(BF16)
        return carry

    lax.fori_loop(0, OWNERS, put, 0)


def second_kernel(
    one_ref, now_ref, speed_ref, source_ref, forward_ref, high_ref, low_ref,
    done_hbm, two_ref, image_ref, ext, zs, sem,
):
    copy = pltpu.make_async_copy(one_ref, done_hbm, sem)
    copy.start()
    depth_terms(one_ref, high_ref, low_ref, zs)
    extend(one_ref, ext)

    def plane(x, carry):
        for ty in range(4):
            rows = slice(8 * ty, 8 * ty + 8)
            summed, middle = laplace_rows(ext, zs, x, ty)
            two = (
                2.0 * middle - now_ref[0, x, rows, :] + speed_ref[0, x, rows, :] * summed
                + source_ref[0, 1, x, rows, :]
            )
            two_ref[0, x, rows, :] = two
            image_ref[0, x, rows, :] = forward_ref[0, 0, x, rows, :] * middle + forward_ref[0, 1, x, rows, :] * two
        return carry

    lax.fori_loop(0, CX, plane, 0)
    copy.wait()


def add_halos(rx0, rx1, ry0, ry1, gx, gy, add):
    row = lax.broadcasted_iota(jnp.int32, (8, CZ), 0)

    def x_side(face, side):
        def rows_of(ty):
            at = pl.ds(pl.multiple_of(8 * ty, 8), 8)
            layers = [face[h, at, :].astype(F32) for h in range(4)]
            for j in range(4):
                if side == 0:
                    term = sum(COEFFS[k - 1] * layers[4 + j - k] for k in range(j + 1, 5))
                    add(j, at, term)
                else:
                    term = sum(COEFFS[k - 1] * layers[k - 1 - j] for k in range(j + 1, 5))
                    add(CX - 1 - j, at, term)

        for ty in range(4):
            rows_of(ty)

    def y_side(face, side):
        def weights(h):
            total = jnp.zeros((8, CZ), F32)
            for j in range(4):
                k = 4 + j - h if side == 0 else h + 1 + j
                if 1 <= k <= 4:
                    at = j if side == 0 else 7 - j
                    total = jnp.where(row == at, COEFFS[k - 1], total)
            return total

        columns = [weights(h) for h in range(4)]

        def plane(x, carry):
            layers = face[x].astype(F32)
            term = sum(columns[h] * jnp.broadcast_to(layers[h : h + 1], (8, CZ)) for h in range(4))
            add(x, slice(0, 8) if side == 0 else slice(24, 32), term)
            return carry

        lax.fori_loop(0, CX, plane, 0)

    @pl.when((gx > 0) & (gx % 2 == 1))
    def _():
        x_side(rx0, 0)

    @pl.when((gx > 0) & (gx % 2 == 0))
    def _():
        x_side(rx1, 0)

    @pl.when((gx < NDEV - 1) & (gx % 2 == 1))
    def _():
        x_side(rx1, 1)

    @pl.when((gx < NDEV - 1) & (gx % 2 == 0))
    def _():
        x_side(rx0, 1)

    @pl.when((gy > 0) & (gy % 2 == 1))
    def _():
        y_side(ry0, 0)

    @pl.when((gy > 0) & (gy % 2 == 0))
    def _():
        y_side(ry1, 0)

    @pl.when((gy < NDEV - 1) & (gy % 2 == 1))
    def _():
        y_side(ry1, 1)

    @pl.when((gy < NDEV - 1) & (gy % 2 == 0))
    def _():
        y_side(ry0, 1)


def first_edge_kernel(where_ref, part_ref, speed_ref, rx0, rx1, ry0, ry1, one_ref, sx0, sx1, sy0, sy1):
    del part_ref
    gx = where_ref[0]
    gy = where_ref[1]

    def add(x, rows, term):
        one_ref[0, x, rows, :] = one_ref[0, x, rows, :] + speed_ref[0, x, rows, :] * term

    add_halos(rx0, rx1, ry0, ry1, gx, gy, add)
    emit_faces(
        lambda side: one_ref[0, 28 * side : 28 * side + 4],
        lambda side: one_ref[0, :, 28 * side : 28 * side + 4, :],
        gx, gy, sx0, sx1, sy0, sy1,
    )


def swap_granules(vals):
    granule = lax.broadcasted_iota(jnp.int32, vals[0].shape, 1) // 16
    vals = list(vals)
    for bit in (1, 2, 4):
        mask = (granule & bit) != 0
        for i in range(8):
            if i & bit:
                continue
            low, high = vals[i], vals[i + bit]
            vals[i] = jnp.where(mask, pltpu.roll(high, 16 * bit, 1), low)
            vals[i + bit] = jnp.where(mask, high, pltpu.roll(low, 128 - 16 * bit, 1))
    return vals


def second_edge_kernel(
    where_ref, at_ref, part_ref, image_in, begun_ref, speed_ref, forward_ref, rx0, rx1, ry0, ry1,
    two_ref, image_ref, out_ref, done_hbm, sem,
):
    del part_ref, image_in, begun_ref
    gx = where_ref[0]
    gy = where_ref[1]

    def add(x, rows, term):
        change = speed_ref[0, x, rows, :] * term
        two_ref[0, x, rows, :] = two_ref[0, x, rows, :] + change
        image_ref[0, x, rows, :] = image_ref[0, x, rows, :] + forward_ref[0, 1, x, rows, :] * change

    add_halos(rx0, rx1, ry0, ry1, gx, gy, add)
    copy = pltpu.make_async_copy(two_ref, done_hbm, sem)
    copy.start()

    def column(tx, carry):
        for pair in range(2):
            for zv in range(4):
                pieces = swap_granules(
                    [
                        image_ref[0, 8 * tx + x, 16 * pair : 16 * pair + 16, 128 * zv : 128 * zv + 128].astype(BF16)
                        for x in range(8)
                    ]
                )
                for p in range(8):
                    for half in range(2):
                        at = at_ref[tx * 128 + (2 * pair + half) * 32 + zv * 8 + p]
                        out_ref[at] = pieces[p][8 * half : 8 * half + 4]
                        out_ref[at + 1] = pieces[p][8 * half + 4 : 8 * half + 8]
        return carry

    lax.fori_loop(0, 4, column, 0)
    copy.wait()


def owner_kernel(in_ref, grad_ref, rows, ids, spread):
    def unpack(j, carry):
        halves = []
        for b in range(2):
            source = 2 * j + b
            for k in range(CAP):
                rows[source * CAP + k, 0:4, :] = in_ref[source * SLABS + 2 * k].astype(F32)
                rows[source * CAP + k, 4:8, :] = in_ref[source * SLABS + 2 * k + 1].astype(F32)
            halves.append(in_ref[source * SLABS + 8].astype(F32))
        ids[pl.ds(8 * j, 8), :] = jnp.concatenate(halves, axis=0)
        return carry

    lax.fori_loop(0, OWNERS // 2, unpack, 0)
    slot = lax.broadcasted_iota(jnp.int32, (OWNERS * CAP, 128), 1).astype(F32)
    onehot = jnp.where(ids[...] == slot, 1.0, 0.0).astype(BF16)
    for y in range(8):
        spread[:, 128 * y : 128 * y + 128] = lax.dot_general(
            onehot, rows[:, y, :].astype(BF16), (((0,), (0,)), ((), ())), preferred_element_type=F32
        )
    for t in range(16):
        at = slice(8 * t, 8 * t + 8)
        vals = swap_granules([spread[at, 128 * y : 128 * y + 128] for y in range(8)])
        for x in range(8):
            grad_ref[at, 128 * x : 128 * x + 128] = vals[x]


SMEM = pl.BlockSpec(memory_space=pltpu.SMEM)
HBM = pl.BlockSpec(memory_space=pl.ANY)
VMEM = pl.BlockSpec(memory_space=pltpu.VMEM)


def params(mib):
    return pltpu.CompilerParams(vmem_limit_bytes=mib * MIB)


def near(array):
    return pltpu.with_memory_space_constraint(array, pltpu.VMEM)


def per_device(
    adjoint_prev, adjoint_now, speed_term, adjoint_source, forward_accel, footprint, live_counts
):
    place = jnp.stack([lax.axis_index("gx"), lax.axis_index("gy")]).astype(jnp.int32)
    faces_out = [pltpu.VMEM((4, CY, CZ), BF16)] * 2 + [pltpu.VMEM((CX, 4, CZ), BF16)] * 2
    level = pltpu.VMEM((1, CX, CY, CZ), F32)
    final = jax.ShapeDtypeStruct((1, CX, CY, CZ), F32)
    begun = pltpu.VMEM((OWNERS * SLABS, 4, 128), BF16)
    ext = pltpu.VMEM((CX + 8, CY + 16, CZ), F32)
    depth = pltpu.VMEM((CX, CY, CZ), F32)

    send = pl.pallas_call(
        face_kernel,
        in_specs=[SMEM, HBM],
        out_specs=[VMEM] * 4,
        out_shape=faces_out,
        scratch_shapes=[
            pltpu.VMEM((2, 4, CY, CZ), F32), pltpu.VMEM((2, CX, 8, CZ), F32), pltpu.SemaphoreType.DMA((4,)),
        ],
        compiler_params=params(8),
        name="faces",
    )(place, adjoint_now)
    faces = swap_faces(*send)
    now = near(adjoint_now)
    prev = near(adjoint_prev)
    speed = near(speed_term)
    source = near(adjoint_source)
    forward = near(forward_accel)
    high, low = [near(jnp.asarray(term)) for term in depth_band()]
    part_one, outgoing, at = pl.pallas_call(
        first_kernel,
        in_specs=[SMEM, SMEM] + [VMEM] * 6,
        out_specs=[VMEM, VMEM, SMEM],
        out_shape=[level, begun, jax.ShapeDtypeStruct((SUB,), jnp.int32)],
        scratch_shapes=[ext, depth, pltpu.VMEM((OWNERS, CAP, 128), F32), pltpu.SMEM((OWNERS,), jnp.int32)],
        compiler_params=params(12),
        name="level_one",
    )(footprint.reshape(-1), live_counts.reshape(-1), now, prev, speed, source, high, low)
    whole_one, *send = pl.pallas_call(
        first_edge_kernel,
        in_specs=[SMEM] + [VMEM] * 6,
        out_specs=[VMEM] * 5,
        out_shape=[level] + faces_out,
        input_output_aliases={1: 0},
        compiler_params=params(4),
        name="level_one_edge",
    )(place, part_one, speed, *[near(face) for face in faces])
    faces = swap_faces(*send)
    level_one, part_two, image = pl.pallas_call(
        second_kernel,
        in_specs=[VMEM] * 7,
        out_specs=[HBM, VMEM, VMEM],
        out_shape=[final, level, level],
        scratch_shapes=[ext, depth, pltpu.SemaphoreType.DMA],
        compiler_params=params(12),
        name="level_two",
    )(whole_one, now, speed, source, forward, high, low)
    _, _, outgoing, level_two = pl.pallas_call(
        second_edge_kernel,
        in_specs=[SMEM, SMEM] + [VMEM] * 9,
        out_specs=[VMEM, VMEM, VMEM, HBM],
        out_shape=[level, level, begun, final],
        scratch_shapes=[pltpu.SemaphoreType.DMA],
        input_output_aliases={2: 0, 3: 1, 4: 2},
        compiler_params=params(4),
        name="level_two_edge",
    )(place, at, part_two, image, outgoing, speed, forward, *[near(face) for face in faces])
    incoming = lax.all_to_all(outgoing, ("shot", "gx", "gy"), split_axis=0, concat_axis=0, tiled=True)
    gradient = pl.pallas_call(
        owner_kernel,
        in_specs=[VMEM],
        out_specs=VMEM,
        out_shape=jax.ShapeDtypeStruct((OWNERS, 1024), F32),
        scratch_shapes=[
            pltpu.VMEM((OWNERS * CAP, 8, 128), F32),
            pltpu.VMEM((OWNERS * CAP, 128), F32),
            pltpu.VMEM((OWNERS, 1024), F32),
        ],
        compiler_params=params(8),
        name="owner_sum",
    )(near(incoming))
    return (level_one, level_two, gradient)


def solution(mesh):
    return jax.shard_map(
        per_device,
        mesh=mesh,
        in_specs=(
            P("shot", "gx", "gy", None),
            P("shot", "gx", "gy", None),
            P("shot", "gx", "gy", None),
            P("shot", None, "gx", "gy", None),
            P("shot", None, "gx", "gy", None),
            P("shot", "gx", "gy", None),
            P("shot", "gx", "gy"),
        ),
        out_specs=(
            P("shot", "gx", "gy", None),
            P("shot", "gx", "gy", None),
            P(("shot", "gx", "gy"), None),
        ),
        check_vma=False,
    )
```

```python
import jax
import jax.numpy as jnp
import numpy as np
from jax import lax
from jax.experimental import pallas as pl
from jax.experimental.pallas import tpu as pltpu
from jax.sharding import PartitionSpec as P

CENTER = -205.0 / 72.0
COEFFS = (8.0 / 5.0, -1.0 / 5.0, 8.0 / 315.0, -1.0 / 560.0)

CX = 32
CY = 32
CZ = 512
OWNERS = 128
CAP = 4
SUB = 512
SLABS = 9
NDEV = 8

F32 = jnp.float32
BF16 = jnp.bfloat16
FACES_FLOPS = 10_000_000_000
MIB = 1024 * 1024

SWAP_A = [(i, i ^ 1) for i in range(NDEV)]
SWAP_B = [(i, (i + 1) % NDEV if i % 2 else (i - 1) % NDEV) for i in range(NDEV)]


def depth_band():
    band = np.zeros((CZ, CZ), np.float64)
    for k, weight in enumerate(COEFFS, 1):
        band += weight * (np.eye(CZ, k=k) + np.eye(CZ, k=-k))
    high = band.astype(jnp.bfloat16)
    low = (band - high.astype(np.float64)).astype(jnp.bfloat16)
    return high, low


def swap_faces(x0, x1, y0, y1):
    return (
        lax.ppermute(x0, "gx", SWAP_A),
        lax.ppermute(x1, "gx", SWAP_B),
        lax.ppermute(y0, "gy", SWAP_A),
        lax.ppermute(y1, "gy", SWAP_B),
    )


def emit_faces(get_x, get_y, gx, gy, sx0, sx1, sy0, sy1):
    @pl.when(gx % 2 == 1)
    def _():
        sx0[...] = get_x(0).astype(BF16)
        sx1[...] = get_x(1).astype(BF16)

    @pl.when(gx % 2 == 0)
    def _():
        sx0[...] = get_x(1).astype(BF16)
        sx1[...] = get_x(0).astype(BF16)

    @pl.when(gy % 2 == 1)
    def _():
        sy0[...] = get_y(0).astype(BF16)
        sy1[...] = get_y(1).astype(BF16)

    @pl.when(gy % 2 == 0)
    def _():
        sy0[...] = get_y(1).astype(BF16)
        sy1[...] = get_y(0).astype(BF16)


def face_kernel(where_ref, now_hbm, sx0, sx1, sy0, sy1, xs, ys, sems):
    gx = where_ref[0]
    gy = where_ref[1]
    copies = [
        pltpu.make_async_copy(now_hbm.at[0, 0:4], xs.at[0], sems.at[0]),
        pltpu.make_async_copy(now_hbm.at[0, 28:32], xs.at[1], sems.at[1]),
        pltpu.make_async_copy(now_hbm.at[0, :, 0:4, :], ys.at[0], sems.at[2]),
        pltpu.make_async_copy(now_hbm.at[0, :, 28:32, :], ys.at[1], sems.at[3]),
    ]
    for copy in copies:
        copy.start()
    for copy in copies:
        copy.wait()
    emit_faces(
        lambda side: xs[side], lambda side: ys[side], gx, gy, sx0, sx1, sy0, sy1
    )


def depth_term(block, high_ref, low_ref):
    block = block.reshape(8 * CY, CZ)
    big = block.astype(BF16)
    small = (block - big.astype(F32)).astype(BF16)
    term = jnp.dot(big, high_ref[...], preferred_element_type=F32)
    term = term + jnp.dot(big, low_ref[...], preferred_element_type=F32)
    term = term + jnp.dot(small, high_ref[...], preferred_element_type=F32)
    return term.reshape(8, CY, CZ)


def clear_edges(ext):
    ext[0:4, 8:40, :] = jnp.zeros((4, CY, CZ), F32)
    ext[36:40, 8:40, :] = jnp.zeros((4, CY, CZ), F32)

    def clear(x, carry):
        ext[x + 4, 0:8, :] = jnp.zeros((8, CZ), F32)
        ext[x + 4, 40:48, :] = jnp.zeros((8, CZ), F32)
        return carry

    lax.fori_loop(0, CX, clear, 0)


def laplace_rows(ext, zs, x, ty):
    rows = ext[x + 4, 8 * ty : 8 * ty + 24, :]
    middle = rows[8:16]
    summed = (3.0 * CENTER) * middle + zs[x, 8 * ty : 8 * ty + 8, :]
    for k, weight in enumerate(COEFFS, 1):
        nearby = ext[x + 4 + k, 8 * ty + 8 : 8 * ty + 16, :] + ext[x + 4 - k, 8 * ty + 8 : 8 * ty + 16, :]
        nearby = nearby + rows[8 + k : 16 + k] + rows[8 - k : 16 - k]
        summed = summed + weight * nearby
    return summed, middle


def place_pieces(foot_ref, live, odd, at_ref, out_ref):
    listed = foot_ref[...]
    owner = listed // OWNERS
    piece = lax.broadcasted_iota(jnp.int32, (1, SUB), 1)
    slot = jnp.where(piece < live, listed % OWNERS, -1)
    match = owner == lax.broadcasted_iota(jnp.int32, (OWNERS, SUB), 0)
    earlier = lax.broadcasted_iota(jnp.int32, (SUB, SUB), 0) < lax.broadcasted_iota(jnp.int32, (SUB, SUB), 1)
    ahead = jnp.dot(
        jnp.where(match, 1.0, 0.0).astype(BF16), jnp.where(earlier, 1.0, 0.0).astype(BF16), preferred_element_type=F32
    )
    rank = jnp.sum(jnp.where(match, ahead, 0.0), axis=0, keepdims=True).astype(jnp.int32)
    at_ref[...] = owner * SLABS + 2 * rank + odd
    order = owner * CAP + rank
    chosen = jnp.where(lax.broadcasted_iota(jnp.int32, (SUB, SUB), 0) == order, 1.0, 0.0).astype(BF16)
    slots = lax.dot_general(
        chosen, jnp.broadcast_to(slot.astype(F32), (OWNERS, SUB)).astype(BF16), (((1,), (1,)), ((), ())),
        preferred_element_type=F32,
    ).astype(BF16)
    for o in range(OWNERS):
        out_ref[o * SLABS + jnp.where(odd == 1, 0, SLABS - 1)] = slots[CAP * o : CAP * o + CAP]


def first_kernel(
    where_ref, live_ref, foot_ref, now_ref, prev_ref, source_ref, speed_ref, high_ref, low_ref,
    one_ref, out_ref, at_ref, ext, zs,
):
    place_pieces(foot_ref, live_ref[0], where_ref[1] % 2, at_ref, out_ref)
    clear_edges(ext)
    for i in range(4):
        block = now_ref[0, 8 * i : 8 * i + 8]
        ext[8 * i + 4 : 8 * i + 12, 8:40, :] = block
        zs[8 * i : 8 * i + 8] = depth_term(block, high_ref, low_ref)

    def plane(x, carry):
        for ty in range(4):
            rows = slice(8 * ty, 8 * ty + 8)
            summed, middle = laplace_rows(ext, zs, x, ty)
            one_ref[0, x, rows, :] = (
                2.0 * middle - prev_ref[0, x, rows, :] + speed_ref[0, x, rows, :] * summed
                + source_ref[0, 0, x, rows, :]
            )
        return carry

    lax.fori_loop(0, CX, plane, 0)


def second_kernel(
    one_ref, now_ref, speed_ref, source_ref, forward_ref, high_ref, low_ref,
    done_hbm, two_ref, image_ref, ext, zs, sem,
):
    copy = pltpu.make_async_copy(one_ref, done_hbm, sem)
    copy.start()
    clear_edges(ext)
    for i in range(4):
        block = one_ref[0, 8 * i : 8 * i + 8]
        ext[8 * i + 4 : 8 * i + 12, 8:40, :] = block
        zs[8 * i : 8 * i + 8] = depth_term(block, high_ref, low_ref)

    def plane(x, carry):
        for ty in range(4):
            rows = slice(8 * ty, 8 * ty + 8)
            summed, middle = laplace_rows(ext, zs, x, ty)
            two = (
                2.0 * middle - now_ref[0, x, rows, :] + speed_ref[0, x, rows, :] * summed
                + source_ref[0, 1, x, rows, :]
            )
            two_ref[0, x, rows, :] = two
            image_ref[0, x, rows, :] = forward_ref[0, 0, x, rows, :] * middle + forward_ref[0, 1, x, rows, :] * two
        return carry

    lax.fori_loop(0, CX, plane, 0)
    copy.wait()


def add_halos(rx0, rx1, ry0, ry1, gx, gy, add):
    row = lax.broadcasted_iota(jnp.int32, (8, CZ), 0)

    def x_side(face, side):
        def rows_of(ty):
            at = pl.ds(pl.multiple_of(8 * ty, 8), 8)
            layers = [face[h, at, :].astype(F32) for h in range(4)]
            for j in range(4):
                if side == 0:
                    term = sum(COEFFS[k - 1] * layers[4 + j - k] for k in range(j + 1, 5))
                    add(j, at, term)
                else:
                    term = sum(COEFFS[k - 1] * layers[k - 1 - j] for k in range(j + 1, 5))
                    add(CX - 1 - j, at, term)

        for ty in range(4):
            rows_of(ty)

    def y_side(face, side):
        def weights(h):
            total = jnp.zeros((8, CZ), F32)
            for j in range(4):
                k = 4 + j - h if side == 0 else h + 1 + j
                if 1 <= k <= 4:
                    at = j if side == 0 else 7 - j
                    total = jnp.where(row == at, COEFFS[k - 1], total)
            return total

        columns = [weights(h) for h in range(4)]

        def plane(x, carry):
            layers = face[x].astype(F32)
            term = sum(columns[h] * jnp.broadcast_to(layers[h : h + 1], (8, CZ)) for h in range(4))
            add(x, slice(0, 8) if side == 0 else slice(24, 32), term)
            return carry

        lax.fori_loop(0, CX, plane, 0)

    @pl.when((gx > 0) & (gx % 2 == 1))
    def _():
        x_side(rx0, 0)

    @pl.when((gx > 0) & (gx % 2 == 0))
    def _():
        x_side(rx1, 0)

    @pl.when((gx < NDEV - 1) & (gx % 2 == 1))
    def _():
        x_side(rx1, 1)

    @pl.when((gx < NDEV - 1) & (gx % 2 == 0))
    def _():
        x_side(rx0, 1)

    @pl.when((gy > 0) & (gy % 2 == 1))
    def _():
        y_side(ry0, 0)

    @pl.when((gy > 0) & (gy % 2 == 0))
    def _():
        y_side(ry1, 0)

    @pl.when((gy < NDEV - 1) & (gy % 2 == 1))
    def _():
        y_side(ry1, 1)

    @pl.when((gy < NDEV - 1) & (gy % 2 == 0))
    def _():
        y_side(ry0, 1)


def first_edge_kernel(where_ref, part_ref, speed_ref, rx0, rx1, ry0, ry1, one_ref, sx0, sx1, sy0, sy1):
    del part_ref
    gx = where_ref[0]
    gy = where_ref[1]

    def add(x, rows, term):
        one_ref[0, x, rows, :] = one_ref[0, x, rows, :] + speed_ref[0, x, rows, :] * term

    add_halos(rx0, rx1, ry0, ry1, gx, gy, add)
    emit_faces(
        lambda side: one_ref[0, 28 * side : 28 * side + 4],
        lambda side: one_ref[0, :, 28 * side : 28 * side + 4, :],
        gx, gy, sx0, sx1, sy0, sy1,
    )


def swap_granules(vals):
    granule = lax.broadcasted_iota(jnp.int32, vals[0].shape, 1) // 16
    vals = list(vals)
    for bit in (1, 2, 4):
        mask = (granule & bit) != 0
        for i in range(8):
            if i & bit:
                continue
            low, high = vals[i], vals[i + bit]
            vals[i] = jnp.where(mask, pltpu.roll(high, 16 * bit, 1), low)
            vals[i + bit] = jnp.where(mask, high, pltpu.roll(low, 128 - 16 * bit, 1))
    return vals


def second_edge_kernel(
    where_ref, at_ref, part_ref, image_in, begun_ref, speed_ref, forward_ref, rx0, rx1, ry0, ry1,
    two_ref, image_ref, out_ref, done_hbm, sem,
):
    del part_ref, image_in, begun_ref
    gx = where_ref[0]
    gy = where_ref[1]

    def add(x, rows, term):
        change = speed_ref[0, x, rows, :] * term
        two_ref[0, x, rows, :] = two_ref[0, x, rows, :] + change
        image_ref[0, x, rows, :] = image_ref[0, x, rows, :] + forward_ref[0, 1, x, rows, :] * change

    add_halos(rx0, rx1, ry0, ry1, gx, gy, add)
    copy = pltpu.make_async_copy(two_ref, done_hbm, sem)
    copy.start()

    def column(tx, carry):
        for pair in range(2):
            for zv in range(4):
                pieces = swap_granules(
                    [
                        image_ref[0, 8 * tx + x, 16 * pair : 16 * pair + 16, 128 * zv : 128 * zv + 128].astype(BF16)
                        for x in range(8)
                    ]
                )
                for p in range(8):
                    for half in range(2):
                        at = at_ref[0, tx * 128 + (2 * pair + half) * 32 + zv * 8 + p]
                        out_ref[at] = pieces[p][8 * half : 8 * half + 4]
                        out_ref[at + 1] = pieces[p][8 * half + 4 : 8 * half + 8]
        return carry

    lax.fori_loop(0, 4, column, 0)
    copy.wait()


def owner_kernel(in_ref, grad_ref, rows, ids, flat, spread):
    def unpack(j, carry):
        for k in range(2 * CAP):
            rows[8 * j + k] = in_ref[SLABS * j + k + k // CAP].astype(F32)
        ids[pl.ds(pl.multiple_of(8 * j, 8), 8), :] = in_ref[SLABS * j + CAP].astype(F32)
        return carry

    lax.fori_loop(0, OWNERS // 2, unpack, 0, unroll=4)
    slot = lax.broadcasted_iota(jnp.int32, (OWNERS * CAP, 128), 1).astype(F32)
    onehot = jnp.where(ids[...] == slot, 1.0, 0.0).astype(BF16)
    for y in range(8):
        flat[:, 128 * y : 128 * y + 128] = rows[:, y, :].astype(BF16)
    spread[...] = lax.dot_general(onehot, flat[...], (((0,), (0,)), ((), ())), preferred_element_type=F32)
    for t in range(16):
        at = slice(8 * t, 8 * t + 8)
        vals = swap_granules([spread[at, 128 * y : 128 * y + 128] for y in range(8)])
        for x in range(8):
            grad_ref[at, 128 * x : 128 * x + 128] = vals[x]


SMEM = pl.BlockSpec(memory_space=pltpu.SMEM)
HBM = pl.BlockSpec(memory_space=pltpu.HBM)
VMEM = pl.BlockSpec(memory_space=pltpu.VMEM)


def params(mib):
    return pltpu.CompilerParams(vmem_limit_bytes=mib * MIB)


def far(array):
    return pltpu.with_memory_space_constraint(array, pltpu.HBM)


def near(array):
    return pltpu.with_memory_space_constraint(array, pltpu.VMEM)


def per_device(
    adjoint_prev, adjoint_now, speed_term, adjoint_source, forward_accel, footprint, live_counts
):
    place = jnp.stack([lax.axis_index("gx"), lax.axis_index("gy")]).astype(jnp.int32)
    faces_out = [pltpu.VMEM((4, CY, CZ), BF16)] * 2 + [pltpu.VMEM((CX, 4, CZ), BF16)] * 2
    level = pltpu.VMEM((1, CX, CY, CZ), F32)
    final = jax.ShapeDtypeStruct((1, CX, CY, CZ), F32)
    begun = pltpu.VMEM((OWNERS * SLABS, 4, 128), BF16)
    ext = pltpu.VMEM((CX + 8, CY + 16, CZ), F32)
    depth = pltpu.VMEM((CX, CY, CZ), F32)

    send = pl.pallas_call(
        face_kernel,
        in_specs=[SMEM, HBM],
        out_specs=[VMEM] * 4,
        out_shape=faces_out,
        scratch_shapes=[
            pltpu.VMEM((2, 4, CY, CZ), F32), pltpu.VMEM((2, CX, 4, CZ), F32), pltpu.SemaphoreType.DMA((4,)),
        ],
        compiler_params=params(8),
        cost_estimate=pl.CostEstimate(flops=FACES_FLOPS, bytes_accessed=1_000_000, transcendentals=0),
        name="faces",
    )(place, far(adjoint_now))
    faces = swap_faces(*send)
    speed = near(speed_term)
    source = near(adjoint_source)
    forward = near(forward_accel)
    now = near(adjoint_now)
    prev = near(adjoint_prev)
    high, low = [near(jnp.asarray(term)) for term in depth_band()]
    part_one, outgoing, at = pl.pallas_call(
        first_kernel,
        in_specs=[SMEM, SMEM] + [VMEM] * 7,
        out_specs=[VMEM] * 3,
        out_shape=[level, begun, jax.ShapeDtypeStruct((1, SUB), jnp.int32)],
        scratch_shapes=[ext, depth],
        compiler_params=params(12),
        name="level_one",
    )(
        place, live_counts.reshape(-1), footprint.reshape(1, SUB), now, prev, source, speed, high, low,
    )
    whole_one, *send = pl.pallas_call(
        first_edge_kernel,
        in_specs=[SMEM] + [VMEM] * 6,
        out_specs=[VMEM] * 5,
        out_shape=[level] + faces_out,
        input_output_aliases={1: 0},
        compiler_params=params(4),
        name="level_one_edge",
    )(place, part_one, speed, *[near(face) for face in faces])
    faces = swap_faces(*send)
    level_one, part_two, image = pl.pallas_call(
        second_kernel,
        in_specs=[VMEM] * 7,
        out_specs=[HBM, VMEM, VMEM],
        out_shape=[final, level, level],
        scratch_shapes=[ext, depth, pltpu.SemaphoreType.DMA],
        compiler_params=params(12),
        name="level_two",
    )(whole_one, now, speed, source, forward, high, low)
    _, _, outgoing, level_two = pl.pallas_call(
        second_edge_kernel,
        in_specs=[SMEM, SMEM] + [VMEM] * 9,
        out_specs=[VMEM, VMEM, VMEM, HBM],
        out_shape=[level, level, begun, final],
        scratch_shapes=[pltpu.SemaphoreType.DMA],
        input_output_aliases={2: 0, 3: 1, 4: 2},
        compiler_params=params(4),
        name="level_two_edge",
    )(place, at, part_two, image, outgoing, speed, forward, *[near(face) for face in faces])
    incoming = lax.all_to_all(outgoing, ("shot", "gx", "gy"), split_axis=0, concat_axis=0, tiled=True)
    gradient = pl.pallas_call(
        owner_kernel,
        in_specs=[VMEM],
        out_specs=VMEM,
        out_shape=jax.ShapeDtypeStruct((OWNERS, 1024), F32),
        scratch_shapes=[
            pltpu.VMEM((OWNERS * CAP, 8, 128), F32),
            pltpu.VMEM((OWNERS * CAP, 128), F32),
            pltpu.VMEM((OWNERS * CAP, 1024), BF16),
            pltpu.VMEM((OWNERS, 1024), F32),
        ],
        compiler_params=params(8),
        name="owner_sum",
    )(near(incoming.reshape(OWNERS * SLABS // 2, 8, 128)))
    return (level_one, level_two, gradient)


def solution(mesh):
    return jax.shard_map(
        per_device,
        mesh=mesh,
        in_specs=(
            P("shot", "gx", "gy", None),
            P("shot", "gx", "gy", None),
            P("shot", "gx", "gy", None),
            P("shot", None, "gx", "gy", None),
            P("shot", None, "gx", "gy", None),
            P("shot", "gx", "gy", None),
            P("shot", "gx", "gy"),
        ),
        out_specs=(
            P("shot", "gx", "gy", None),
            P("shot", "gx", "gy", None),
            P(("shot", "gx", "gy"), None),
        ),
        check_vma=False,
    )
```

```python
import jax
import jax.numpy as jnp
import numpy as np
from jax import lax
from jax.experimental import pallas as pl
from jax.experimental.pallas import tpu as pltpu
from jax.sharding import PartitionSpec as P

CENTER = -205.0 / 72.0
COEFFS = (8.0 / 5.0, -1.0 / 5.0, 8.0 / 315.0, -1.0 / 560.0)

CX = 32
CY = 32
CZ = 512
OWNERS = 128
CAP = 4
SUB = 512
SLABS = 9
NDEV = 8

F32 = jnp.float32
BF16 = jnp.bfloat16
FACES_FLOPS = 10_000_000_000
MIB = 1024 * 1024

SWAP_A = [(i, i ^ 1) for i in range(NDEV)]
SWAP_B = [(i, (i + 1) % NDEV if i % 2 else (i - 1) % NDEV) for i in range(NDEV)]


def depth_band():
    band = np.zeros((CZ, CZ), np.float64)
    for k, weight in enumerate(COEFFS, 1):
        band += weight * (np.eye(CZ, k=k) + np.eye(CZ, k=-k))
    high = band.astype(jnp.bfloat16)
    low = (band - high.astype(np.float64)).astype(jnp.bfloat16)
    return high, low


def swap_faces(x0, x1, y0, y1):
    return (
        lax.ppermute(x0, "gx", SWAP_A),
        lax.ppermute(x1, "gx", SWAP_B),
        lax.ppermute(y0, "gy", SWAP_A),
        lax.ppermute(y1, "gy", SWAP_B),
    )


def emit_faces(get_x, get_y, gx, gy, sx0, sx1, sy0, sy1):
    @pl.when(gx % 2 == 1)
    def _():
        sx0[...] = get_x(0).astype(BF16)
        sx1[...] = get_x(1).astype(BF16)

    @pl.when(gx % 2 == 0)
    def _():
        sx0[...] = get_x(1).astype(BF16)
        sx1[...] = get_x(0).astype(BF16)

    @pl.when(gy % 2 == 1)
    def _():
        sy0[...] = get_y(0).astype(BF16)
        sy1[...] = get_y(1).astype(BF16)

    @pl.when(gy % 2 == 0)
    def _():
        sy0[...] = get_y(1).astype(BF16)
        sy1[...] = get_y(0).astype(BF16)


def face_kernel(where_ref, now_hbm, sx0, sx1, sy0, sy1, xs, ys, sems):
    gx = where_ref[0]
    gy = where_ref[1]
    copies = [
        pltpu.make_async_copy(now_hbm.at[0, 0:4], xs.at[0], sems.at[0]),
        pltpu.make_async_copy(now_hbm.at[0, 28:32], xs.at[1], sems.at[1]),
        pltpu.make_async_copy(now_hbm.at[0, :, 0:4, :], ys.at[0], sems.at[2]),
        pltpu.make_async_copy(now_hbm.at[0, :, 28:32, :], ys.at[1], sems.at[3]),
    ]
    for copy in copies:
        copy.start()
    for copy in copies:
        copy.wait()
    emit_faces(
        lambda side: xs[side], lambda side: ys[side], gx, gy, sx0, sx1, sy0, sy1
    )


def depth_term(block, high_ref, low_ref):
    block = block.reshape(8 * CY, CZ)
    big = block.astype(BF16)
    small = (block - big.astype(F32)).astype(BF16)
    term = jnp.dot(big, high_ref[...], preferred_element_type=F32)
    term = term + jnp.dot(big, low_ref[...], preferred_element_type=F32)
    term = term + jnp.dot(small, high_ref[...], preferred_element_type=F32)
    return term.reshape(8, CY, CZ)


def clear_edges(ext):
    ext[0:4, 8:40, :] = jnp.zeros((4, CY, CZ), F32)
    ext[36:40, 8:40, :] = jnp.zeros((4, CY, CZ), F32)

    def clear(x, carry):
        ext[x + 4, 0:8, :] = jnp.zeros((8, CZ), F32)
        ext[x + 4, 40:48, :] = jnp.zeros((8, CZ), F32)
        return carry

    lax.fori_loop(0, CX, clear, 0)


def laplace_rows(ext, zs, x, ty):
    rows = ext[x + 4, 8 * ty : 8 * ty + 24, :]
    middle = rows[8:16]
    summed = (3.0 * CENTER) * middle + zs[x, 8 * ty : 8 * ty + 8, :]
    for k, weight in enumerate(COEFFS, 1):
        nearby = ext[x + 4 + k, 8 * ty + 8 : 8 * ty + 16, :] + ext[x + 4 - k, 8 * ty + 8 : 8 * ty + 16, :]
        nearby = nearby + rows[8 + k : 16 + k] + rows[8 - k : 16 - k]
        summed = summed + weight * nearby
    return summed, middle


def place_pieces(foot_ref, live, odd, at_ref, out_ref):
    listed = foot_ref[...]
    owner = listed // OWNERS
    piece = lax.broadcasted_iota(jnp.int32, (1, SUB), 1)
    slot = jnp.where(piece < live, listed % OWNERS, -1)
    match = owner == lax.broadcasted_iota(jnp.int32, (OWNERS, SUB), 0)
    earlier = lax.broadcasted_iota(jnp.int32, (SUB, SUB), 0) < lax.broadcasted_iota(jnp.int32, (SUB, SUB), 1)
    ahead = jnp.dot(
        jnp.where(match, 1.0, 0.0).astype(BF16), jnp.where(earlier, 1.0, 0.0).astype(BF16), preferred_element_type=F32
    )
    rank = jnp.sum(jnp.where(match, ahead, 0.0), axis=0, keepdims=True).astype(jnp.int32)
    at_ref[...] = owner * SLABS + 2 * rank + odd
    order = owner * CAP + rank
    chosen = jnp.where(lax.broadcasted_iota(jnp.int32, (SUB, SUB), 0) == order, 1.0, 0.0).astype(BF16)
    slots = lax.dot_general(
        chosen, jnp.broadcast_to(slot.astype(F32), (OWNERS, SUB)).astype(BF16), (((1,), (1,)), ((), ())),
        preferred_element_type=F32,
    ).astype(BF16)
    for o in range(OWNERS):
        out_ref[o * SLABS + jnp.where(odd == 1, 0, SLABS - 1)] = slots[CAP * o : CAP * o + CAP]


def first_kernel(
    now_ref, prev_ref, source_ref, speed_ref, high_ref, low_ref, one_ref, ext, zs,
):
    clear_edges(ext)
    for i in range(4):
        block = now_ref[0, 8 * i : 8 * i + 8]
        ext[8 * i + 4 : 8 * i + 12, 8:40, :] = block
        zs[8 * i : 8 * i + 8] = depth_term(block, high_ref, low_ref)

    def plane(x, carry):
        for ty in range(4):
            rows = slice(8 * ty, 8 * ty + 8)
            summed, middle = laplace_rows(ext, zs, x, ty)
            one_ref[0, x, rows, :] = (
                2.0 * middle - prev_ref[0, x, rows, :] + speed_ref[0, x, rows, :] * summed
                + source_ref[0, 0, x, rows, :]
            )
        return carry

    lax.fori_loop(0, CX, plane, 0)


def second_kernel(
    where_ref, live_ref, foot_ref, one_ref, now_ref, speed_ref, source_ref, forward_ref, high_ref, low_ref,
    done_hbm, two_ref, image_ref, out_ref, at_ref, ext, zs, sem,
):
    copy = pltpu.make_async_copy(one_ref, done_hbm, sem)
    copy.start()
    place_pieces(foot_ref, live_ref[0], where_ref[1] % 2, at_ref, out_ref)
    clear_edges(ext)
    for i in range(4):
        block = one_ref[0, 8 * i : 8 * i + 8]
        ext[8 * i + 4 : 8 * i + 12, 8:40, :] = block
        zs[8 * i : 8 * i + 8] = depth_term(block, high_ref, low_ref)

    def plane(x, carry):
        for ty in range(4):
            rows = slice(8 * ty, 8 * ty + 8)
            summed, middle = laplace_rows(ext, zs, x, ty)
            two = (
                2.0 * middle - now_ref[0, x, rows, :] + speed_ref[0, x, rows, :] * summed
                + source_ref[0, 1, x, rows, :]
            )
            two_ref[0, x, rows, :] = two
            image_ref[0, x, rows, :] = forward_ref[0, 0, x, rows, :] * middle + forward_ref[0, 1, x, rows, :] * two
        return carry

    lax.fori_loop(0, CX, plane, 0)
    copy.wait()


def add_halos(rx0, rx1, ry0, ry1, gx, gy, update):
    def store(changes):
        for ref, at, value in changes:
            ref[at] = value

    def x_sides(low, high):
        inside = [jnp.where(gx > 0, 1.0, 0.0), jnp.where(gx < NDEV - 1, 1.0, 0.0)]

        def strip(ty, carry):
            rows = pl.ds(pl.multiple_of(8 * ty, 8), 8)
            for side, face in enumerate((low, high)):
                layers = [face[h, rows, :].astype(F32) * inside[side] for h in range(4)]
                changes = []
                for j in range(4):
                    near_first = layers[::-1] if side == 0 else layers
                    term = sum(COEFFS[j + h] * near_first[h] for h in range(4 - j))
                    changes += update(j if side == 0 else CX - 1 - j, rows, slice(0, CZ), term)
                store(changes)
            return carry

        lax.fori_loop(0, 4, strip, 0)

    def y_sides(low, high):
        inside = [jnp.where(gy > 0, 1.0, 0.0), jnp.where(gy < NDEV - 1, 1.0, 0.0)]
        row = lax.broadcasted_iota(jnp.int32, (8, 128), 0)

        def column(side, h):
            total = jnp.zeros((8, 128), F32)
            for j in range(4):
                k = 4 + j - h if side == 0 else h + 1 + j
                if k <= 4:
                    total = jnp.where(row == (j if side == 0 else 7 - j), COEFFS[k - 1] * inside[side], total)
            return total

        columns = [[column(side, h) for h in range(4)] for side in range(2)]

        def planes(i, carry):
            changes = []
            for b in range(4):
                x = 4 * i + b
                for side, face in enumerate((low, high)):
                    layers = face[x].astype(F32)
                    for zv in range(4):
                        lanes = slice(128 * zv, 128 * zv + 128)
                        term = sum(
                            columns[side][h] * jnp.broadcast_to(layers[h : h + 1, lanes], (8, 128)) for h in range(4)
                        )
                        changes += update(x, slice(24 * side, 24 * side + 8), lanes, term)
            store(changes)
            return carry

        lax.fori_loop(0, CX // 4, planes, 0)

    @pl.when(gx % 2 == 1)
    def _():
        x_sides(rx0, rx1)

    @pl.when(gx % 2 == 0)
    def _():
        x_sides(rx1, rx0)

    @pl.when(gy % 2 == 1)
    def _():
        y_sides(ry0, ry1)

    @pl.when(gy % 2 == 0)
    def _():
        y_sides(ry1, ry0)


def first_edge_kernel(where_ref, part_ref, speed_ref, ry1, ry0, rx1, rx0, one_ref, sx0, sx1, sy0, sy1):
    del part_ref
    gx = where_ref[0]
    gy = where_ref[1]

    def update(x, rows, lanes, term):
        at = (0, x, rows, lanes)
        return [(one_ref, at, one_ref[at] + speed_ref[at] * term)]

    add_halos(rx0, rx1, ry0, ry1, gx, gy, update)
    emit_faces(
        lambda side: one_ref[0, 28 * side : 28 * side + 4],
        lambda side: one_ref[0, :, 28 * side : 28 * side + 4, :],
        gx, gy, sx0, sx1, sy0, sy1,
    )


def swap_granules(vals):
    granule = lax.broadcasted_iota(jnp.int32, vals[0].shape, 1) // 16
    vals = list(vals)
    for bit in (1, 2, 4):
        mask = (granule & bit) != 0
        for i in range(8):
            if i & bit:
                continue
            low, high = vals[i], vals[i + bit]
            vals[i] = jnp.where(mask, pltpu.roll(high, 16 * bit, 1), low)
            vals[i + bit] = jnp.where(mask, high, pltpu.roll(low, 128 - 16 * bit, 1))
    return vals


def second_edge_kernel(
    where_ref, at_ref, part_ref, image_in, begun_ref, speed_ref, forward_ref, ry1, ry0, rx1, rx0,
    two_ref, image_ref, out_ref, done_hbm, sem,
):
    del part_ref, image_in, begun_ref
    gx = where_ref[0]
    gy = where_ref[1]

    def update(x, rows, lanes, term):
        at = (0, x, rows, lanes)
        change = speed_ref[at] * term
        return [
            (two_ref, at, two_ref[at] + change),
            (image_ref, at, image_ref[at] + forward_ref[0, 1, x, rows, lanes] * change),
        ]

    add_halos(rx0, rx1, ry0, ry1, gx, gy, update)
    copy = pltpu.make_async_copy(two_ref, done_hbm, sem)
    copy.start()

    def column(tx, carry):
        for pair in range(2):
            for zv in range(4):
                pieces = swap_granules(
                    [
                        image_ref[0, 8 * tx + x, 16 * pair : 16 * pair + 16, 128 * zv : 128 * zv + 128].astype(BF16)
                        for x in range(8)
                    ]
                )
                for p in range(8):
                    for half in range(2):
                        at = at_ref[0, tx * 128 + (2 * pair + half) * 32 + zv * 8 + p]
                        out_ref[at] = pieces[p][8 * half : 8 * half + 4]
                        out_ref[at + 1] = pieces[p][8 * half + 4 : 8 * half + 8]
        return carry

    lax.fori_loop(0, 4, column, 0)
    copy.wait()


def owner_kernel(in_ref, grad_ref, rows, ids, flat, spread):
    def unpack(j, carry):
        for k in range(2 * CAP):
            rows[8 * j + k] = in_ref[SLABS * j + k + k // CAP].astype(F32)
        ids[pl.ds(pl.multiple_of(8 * j, 8), 8), :] = in_ref[SLABS * j + CAP].astype(F32)
        return carry

    lax.fori_loop(0, OWNERS // 2, unpack, 0, unroll=4)
    slot = lax.broadcasted_iota(jnp.int32, (OWNERS * CAP, 128), 1).astype(F32)
    onehot = jnp.where(ids[...] == slot, 1.0, 0.0).astype(BF16)
    for y in range(8):
        flat[:, 128 * y : 128 * y + 128] = rows[:, y, :].astype(BF16)
    spread[...] = lax.dot_general(onehot, flat[...], (((0,), (0,)), ((), ())), preferred_element_type=F32)
    for t in range(16):
        at = slice(8 * t, 8 * t + 8)
        vals = swap_granules([spread[at, 128 * y : 128 * y + 128] for y in range(8)])
        for x in range(8):
            grad_ref[at, 128 * x : 128 * x + 128] = vals[x]


SMEM = pl.BlockSpec(memory_space=pltpu.SMEM)
HBM = pl.BlockSpec(memory_space=pltpu.HBM)
VMEM = pl.BlockSpec(memory_space=pltpu.VMEM)


def params(mib):
    return pltpu.CompilerParams(vmem_limit_bytes=mib * MIB)


def far(array):
    return pltpu.with_memory_space_constraint(array, pltpu.HBM)


def near(array):
    return pltpu.with_memory_space_constraint(array, pltpu.VMEM)


def per_device(
    adjoint_prev, adjoint_now, speed_term, adjoint_source, forward_accel, footprint, live_counts
):
    place = jnp.stack([lax.axis_index("gx"), lax.axis_index("gy")]).astype(jnp.int32)
    faces_out = [pltpu.VMEM((4, CY, CZ), BF16)] * 2 + [pltpu.VMEM((CX, 4, CZ), BF16)] * 2
    level = pltpu.VMEM((1, CX, CY, CZ), F32)
    final = jax.ShapeDtypeStruct((1, CX, CY, CZ), F32)
    begun = pltpu.VMEM((OWNERS * SLABS, 4, 128), BF16)
    ext = pltpu.VMEM((CX + 8, CY + 16, CZ), F32)
    depth = pltpu.VMEM((CX, CY, CZ), F32)

    send = pl.pallas_call(
        face_kernel,
        in_specs=[SMEM, HBM],
        out_specs=[VMEM] * 4,
        out_shape=faces_out,
        scratch_shapes=[
            pltpu.VMEM((2, 4, CY, CZ), F32), pltpu.VMEM((2, CX, 4, CZ), F32), pltpu.SemaphoreType.DMA((4,)),
        ],
        compiler_params=params(8),
        cost_estimate=pl.CostEstimate(flops=FACES_FLOPS, bytes_accessed=1_000_000, transcendentals=0),
        name="faces",
    )(place, far(adjoint_now))
    faces = swap_faces(*send)
    speed = near(speed_term)
    source = near(adjoint_source)
    forward = near(forward_accel)
    now = near(adjoint_now)
    prev = near(adjoint_prev)
    high, low = [near(jnp.asarray(term)) for term in depth_band()]
    part_one = pl.pallas_call(
        first_kernel,
        in_specs=[VMEM] * 6,
        out_specs=VMEM,
        out_shape=level,
        scratch_shapes=[ext, depth],
        compiler_params=params(12),
        name="level_one",
    )(now, prev, source, speed, high, low)
    whole_one, *send = pl.pallas_call(
        first_edge_kernel,
        in_specs=[SMEM] + [VMEM] * 6,
        out_specs=[VMEM] * 5,
        out_shape=[level] + faces_out,
        input_output_aliases={1: 0},
        compiler_params=params(4),
        name="level_one_edge",
    )(place, part_one, speed, *[near(face) for face in faces[::-1]])
    faces = swap_faces(*send)
    level_one, part_two, image, outgoing, at = pl.pallas_call(
        second_kernel,
        in_specs=[SMEM, SMEM] + [VMEM] * 8,
        out_specs=[HBM] + [VMEM] * 4,
        out_shape=[final, level, level, begun, jax.ShapeDtypeStruct((1, SUB), jnp.int32)],
        scratch_shapes=[ext, depth, pltpu.SemaphoreType.DMA],
        compiler_params=params(12),
        name="level_two",
    )(
        place, live_counts.reshape(-1), footprint.reshape(1, SUB),
        whole_one, now, speed, source, forward, high, low,
    )
    _, _, outgoing, level_two = pl.pallas_call(
        second_edge_kernel,
        in_specs=[SMEM, SMEM] + [VMEM] * 9,
        out_specs=[VMEM, VMEM, VMEM, HBM],
        out_shape=[level, level, begun, final],
        scratch_shapes=[pltpu.SemaphoreType.DMA],
        input_output_aliases={2: 0, 3: 1, 4: 2},
        compiler_params=params(4),
        name="level_two_edge",
    )(place, at, part_two, image, outgoing, speed, forward, *[near(face) for face in faces[::-1]])
    incoming = lax.all_to_all(outgoing, ("shot", "gx", "gy"), split_axis=0, concat_axis=0, tiled=True)
    gradient = pl.pallas_call(
        owner_kernel,
        in_specs=[VMEM],
        out_specs=VMEM,
        out_shape=jax.ShapeDtypeStruct((OWNERS, 1024), F32),
        scratch_shapes=[
            pltpu.VMEM((OWNERS * CAP, 8, 128), F32),
            pltpu.VMEM((OWNERS * CAP, 128), F32),
            pltpu.VMEM((OWNERS * CAP, 1024), BF16),
            pltpu.VMEM((OWNERS, 1024), F32),
        ],
        compiler_params=params(8),
        name="owner_sum",
    )(near(incoming.reshape(OWNERS * SLABS // 2, 8, 128)))
    return (level_one, level_two, gradient)


def solution(mesh):
    return jax.shard_map(
        per_device,
        mesh=mesh,
        in_specs=(
            P("shot", "gx", "gy", None),
            P("shot", "gx", "gy", None),
            P("shot", "gx", "gy", None),
            P("shot", None, "gx", "gy", None),
            P("shot", None, "gx", "gy", None),
            P("shot", "gx", "gy", None),
            P("shot", "gx", "gy"),
        ),
        out_specs=(
            P("shot", "gx", "gy", None),
            P("shot", "gx", "gy", None),
            P(("shot", "gx", "gy"), None),
        ),
        check_vma=False,
    )
```

```python
import jax
import jax.numpy as jnp
import numpy as np
from jax import lax
from jax.experimental import pallas as pl
from jax.experimental.pallas import tpu as pltpu
from jax.sharding import PartitionSpec as P

CENTER = -205.0 / 72.0
COEFFS = (8.0 / 5.0, -1.0 / 5.0, 8.0 / 315.0, -1.0 / 560.0)

CX = 32
CY = 32
CZ = 512
OWNERS = 128
CAP = 4
SUB = 512
SLABS = 9
NDEV = 8

F32 = jnp.float32
BF16 = jnp.bfloat16
FACES_FLOPS = 10_000_000_000
MIB = 1024 * 1024

SWAP_A = [(i, i ^ 1) for i in range(NDEV)]
SWAP_B = [(i, (i + 1) % NDEV if i % 2 else (i - 1) % NDEV) for i in range(NDEV)]


def banded(size, block):
    band = np.zeros((block, block), np.float64)
    for k, weight in enumerate(COEFFS, 1):
        band += weight * (np.eye(block, k=k) + np.eye(block, k=-k))
    band = np.kron(np.eye(size // block), band)
    high = band.astype(jnp.bfloat16)
    low = (band - high.astype(np.float64)).astype(jnp.bfloat16)
    return high, low


def swap_faces(x0, x1, y0, y1):
    return (
        lax.ppermute(x0, "gx", SWAP_A),
        lax.ppermute(x1, "gx", SWAP_B),
        lax.ppermute(y0, "gy", SWAP_A),
        lax.ppermute(y1, "gy", SWAP_B),
    )


def emit_faces(get_x, get_y, gx, gy, sx0, sx1, sy0, sy1):
    @pl.when(gx % 2 == 1)
    def _():
        sx0[...] = get_x(0).astype(BF16)
        sx1[...] = get_x(1).astype(BF16)

    @pl.when(gx % 2 == 0)
    def _():
        sx0[...] = get_x(1).astype(BF16)
        sx1[...] = get_x(0).astype(BF16)

    @pl.when(gy % 2 == 1)
    def _():
        sy0[...] = get_y(0).astype(BF16)
        sy1[...] = get_y(1).astype(BF16)

    @pl.when(gy % 2 == 0)
    def _():
        sy0[...] = get_y(1).astype(BF16)
        sy1[...] = get_y(0).astype(BF16)


def face_kernel(where_ref, now_hbm, sx0, sx1, sy0, sy1, xs, ys, sems):
    gx = where_ref[0]
    gy = where_ref[1]
    copies = [
        pltpu.make_async_copy(now_hbm.at[0, 0:4], xs.at[0], sems.at[0]),
        pltpu.make_async_copy(now_hbm.at[0, 28:32], xs.at[1], sems.at[1]),
        pltpu.make_async_copy(now_hbm.at[0, :, 0:4, :], ys.at[0], sems.at[2]),
        pltpu.make_async_copy(now_hbm.at[0, :, 28:32, :], ys.at[1], sems.at[3]),
    ]
    for copy in copies:
        copy.start()
    for copy in copies:
        copy.wait()
    emit_faces(
        lambda side: xs[side], lambda side: ys[side], gx, gy, sx0, sx1, sy0, sy1
    )


def plane_terms(block, bands):
    high, low, row_high, row_low = bands
    block = block.reshape(8 * CY, CZ)
    big = block.astype(BF16)
    small = (block - big.astype(F32)).astype(BF16)
    term = jnp.dot(big, high[...], preferred_element_type=F32)
    term = term + jnp.dot(big, low[...], preferred_element_type=F32)
    term = term + jnp.dot(small, high[...], preferred_element_type=F32)
    term = term + jnp.dot(row_high[...], big, preferred_element_type=F32)
    term = term + jnp.dot(row_low[...], big, preferred_element_type=F32)
    term = term + jnp.dot(row_high[...], small, preferred_element_type=F32)
    return term.reshape(8, CY, CZ)


def prepare(values, ext, zs, bands):
    ext[0:4] = jnp.zeros((4, CY, CZ), F32)
    ext[36:40] = jnp.zeros((4, CY, CZ), F32)
    for i in range(4):
        block = values[0, 8 * i : 8 * i + 8]
        ext[8 * i + 4 : 8 * i + 12] = block
        zs[8 * i : 8 * i + 8] = plane_terms(block, bands)


def laplace_rows(ext, zs, x, ty):
    rows = slice(8 * ty, 8 * ty + 8)
    middle = ext[x + 4, rows, :]
    summed = (3.0 * CENTER) * middle + zs[x, rows, :]
    for k, weight in enumerate(COEFFS, 1):
        summed = summed + weight * (ext[x + 4 + k, rows, :] + ext[x + 4 - k, rows, :])
    return summed, middle


def place_pieces(foot_ref, live, odd, at_ref, out_ref):
    listed = foot_ref[...]
    owner = listed // OWNERS
    piece = lax.broadcasted_iota(jnp.int32, (1, SUB), 1)
    slot = jnp.where(piece < live, listed % OWNERS, -1)
    match = owner == lax.broadcasted_iota(jnp.int32, (OWNERS, SUB), 0)
    earlier = lax.broadcasted_iota(jnp.int32, (SUB, SUB), 0) < lax.broadcasted_iota(jnp.int32, (SUB, SUB), 1)
    ahead = jnp.dot(
        jnp.where(match, 1.0, 0.0).astype(BF16), jnp.where(earlier, 1.0, 0.0).astype(BF16), preferred_element_type=F32
    )
    rank = jnp.sum(jnp.where(match, ahead, 0.0), axis=0, keepdims=True).astype(jnp.int32)
    at_ref[...] = owner * SLABS + 2 * rank + odd
    order = owner * CAP + rank
    chosen = jnp.where(lax.broadcasted_iota(jnp.int32, (SUB, SUB), 0) == order, 1.0, 0.0).astype(BF16)
    slots = lax.dot_general(
        chosen, jnp.broadcast_to(slot.astype(F32), (OWNERS, SUB)).astype(BF16), (((1,), (1,)), ((), ())),
        preferred_element_type=F32,
    ).astype(BF16)
    for o in range(OWNERS):
        out_ref[o * SLABS + jnp.where(odd == 1, 0, SLABS - 1)] = slots[CAP * o : CAP * o + CAP]


def first_kernel(
    now_ref, prev_ref, source_ref, speed_ref, high, low, row_high, row_low, one_ref, ext, zs,
):
    bands = (high, low, row_high, row_low)
    prepare(now_ref, ext, zs, bands)

    def plane(x, carry):
        for ty in range(4):
            rows = slice(8 * ty, 8 * ty + 8)
            summed, middle = laplace_rows(ext, zs, x, ty)
            one_ref[0, x, rows, :] = (
                2.0 * middle - prev_ref[0, x, rows, :] + speed_ref[0, x, rows, :] * summed
                + source_ref[0, 0, x, rows, :]
            )
        return carry

    lax.fori_loop(0, CX, plane, 0)


def second_kernel(
    where_ref, foot_ref, one_ref, now_ref, speed_ref, source_ref, forward_ref, high, low, row_high, row_low,
    done_hbm, two_ref, image_ref, out_ref, at_ref, ext, zs, sem,
):
    bands = (high, low, row_high, row_low)
    copy = pltpu.make_async_copy(one_ref, done_hbm, sem)
    copy.start()
    place_pieces(foot_ref, where_ref[2], where_ref[1] % 2, at_ref, out_ref)
    prepare(one_ref, ext, zs, bands)

    def plane(x, carry):
        for ty in range(4):
            rows = slice(8 * ty, 8 * ty + 8)
            summed, middle = laplace_rows(ext, zs, x, ty)
            two = (
                2.0 * middle - now_ref[0, x, rows, :] + speed_ref[0, x, rows, :] * summed
                + source_ref[0, 1, x, rows, :]
            )
            two_ref[0, x, rows, :] = two
            image_ref[0, x, rows, :] = forward_ref[0, 0, x, rows, :] * middle + forward_ref[0, 1, x, rows, :] * two
        return carry

    lax.fori_loop(0, CX, plane, 0)
    copy.wait()


def add_halos(rx0, rx1, ry0, ry1, gx, gy, update):
    def store(changes):
        for ref, at, value in changes:
            ref[at] = value

    def x_sides(low, high):
        inside = [jnp.where(gx > 0, 1.0, 0.0), jnp.where(gx < NDEV - 1, 1.0, 0.0)]

        def strip(ty, carry):
            rows = pl.ds(pl.multiple_of(8 * ty, 8), 8)
            for side, face in enumerate((low, high)):
                layers = [face[h, rows, :].astype(F32) * inside[side] for h in range(4)]
                changes = []
                for j in range(4):
                    near_first = layers[::-1] if side == 0 else layers
                    term = sum(COEFFS[j + h] * near_first[h] for h in range(4 - j))
                    changes += update(j if side == 0 else CX - 1 - j, rows, slice(0, CZ), term)
                store(changes)
            return carry

        lax.fori_loop(0, 4, strip, 0)

    def y_sides(low, high):
        inside = [jnp.where(gy > 0, 1.0, 0.0), jnp.where(gy < NDEV - 1, 1.0, 0.0)]
        row = lax.broadcasted_iota(jnp.int32, (8, 128), 0)

        def column(side, h):
            total = jnp.zeros((8, 128), F32)
            for j in range(4):
                k = 4 + j - h if side == 0 else h + 1 + j
                if k <= 4:
                    total = jnp.where(row == (j if side == 0 else 7 - j), COEFFS[k - 1] * inside[side], total)
            return total

        columns = [[column(side, h) for h in range(4)] for side in range(2)]

        def planes(i, carry):
            changes = []
            for b in range(4):
                x = 4 * i + b
                for side, face in enumerate((low, high)):
                    layers = face[x].astype(F32)
                    for zv in range(4):
                        lanes = slice(128 * zv, 128 * zv + 128)
                        term = sum(
                            columns[side][h] * jnp.broadcast_to(layers[h : h + 1, lanes], (8, 128)) for h in range(4)
                        )
                        changes += update(x, slice(24 * side, 24 * side + 8), lanes, term)
            store(changes)
            return carry

        lax.fori_loop(0, CX // 4, planes, 0)

    @pl.when(gx % 2 == 1)
    def _():
        x_sides(rx0, rx1)

    @pl.when(gx % 2 == 0)
    def _():
        x_sides(rx1, rx0)

    @pl.when(gy % 2 == 1)
    def _():
        y_sides(ry0, ry1)

    @pl.when(gy % 2 == 0)
    def _():
        y_sides(ry1, ry0)


def first_edge_kernel(where_ref, part_ref, speed_ref, ry1, ry0, rx1, rx0, one_ref, sx0, sx1, sy0, sy1):
    del part_ref
    gx = where_ref[0]
    gy = where_ref[1]

    def update(x, rows, lanes, term):
        at = (0, x, rows, lanes)
        return [(one_ref, at, one_ref[at] + speed_ref[at] * term)]

    add_halos(rx0, rx1, ry0, ry1, gx, gy, update)
    emit_faces(
        lambda side: one_ref[0, 28 * side : 28 * side + 4],
        lambda side: one_ref[0, :, 28 * side : 28 * side + 4, :],
        gx, gy, sx0, sx1, sy0, sy1,
    )


def swap_granules(vals):
    granule = lax.broadcasted_iota(jnp.int32, vals[0].shape, 1) // 16
    vals = list(vals)
    for bit in (1, 2, 4):
        mask = (granule & bit) != 0
        for i in range(8):
            if i & bit:
                continue
            low, high = vals[i], vals[i + bit]
            vals[i] = jnp.where(mask, pltpu.roll(high, 16 * bit, 1), low)
            vals[i + bit] = jnp.where(mask, high, pltpu.roll(low, 128 - 16 * bit, 1))
    return vals


def second_edge_kernel(
    where_ref, at_ref, part_ref, image_in, begun_ref, speed_ref, forward_ref, ry1, ry0, rx1, rx0,
    two_ref, image_ref, out_ref, done_hbm, sem,
):
    del part_ref, image_in, begun_ref
    gx = where_ref[0]
    gy = where_ref[1]

    def update(x, rows, lanes, term):
        at = (0, x, rows, lanes)
        change = speed_ref[at] * term
        return [
            (two_ref, at, two_ref[at] + change),
            (image_ref, at, image_ref[at] + forward_ref[0, 1, x, rows, lanes] * change),
        ]

    add_halos(rx0, rx1, ry0, ry1, gx, gy, update)
    copy = pltpu.make_async_copy(two_ref, done_hbm, sem)
    copy.start()

    def column(tx, carry):
        for pair in range(2):
            for zv in range(4):
                pieces = swap_granules(
                    [
                        image_ref[0, 8 * tx + x, 16 * pair : 16 * pair + 16, 128 * zv : 128 * zv + 128].astype(BF16)
                        for x in range(8)
                    ]
                )
                for p in range(8):
                    for half in range(2):
                        at = at_ref[0, tx * 128 + (2 * pair + half) * 32 + zv * 8 + p]
                        out_ref[at] = pieces[p][8 * half : 8 * half + 4]
                        out_ref[at + 1] = pieces[p][8 * half + 4 : 8 * half + 8]
        return carry

    lax.fori_loop(0, 4, column, 0)
    copy.wait()


def owner_kernel(in_ref, grad_ref, ids, flat, spread):
    def unpack(j, carry):
        lines = []
        slots = []
        for b in range(2):
            base = SLABS * (2 * j + b)
            pieces = [in_ref[base + k + k // CAP].astype(F32) for k in range(2 * CAP)]
            lines.append(jnp.swapaxes(jnp.stack(pieces), 0, 1))
            slots.append(in_ref[base + CAP].astype(F32))
        at = pl.ds(pl.multiple_of(16 * j, 16), 16)
        for y in range(8):
            flat[at, 128 * y : 128 * y + 128] = jnp.concatenate([lines[0][y], lines[1][y]], axis=0).astype(BF16)
        ids[at, :] = jnp.concatenate(slots, axis=0)
        return carry

    lax.fori_loop(0, OWNERS // 4, unpack, 0, unroll=4)
    slot = lax.broadcasted_iota(jnp.int32, (OWNERS * CAP, 128), 1).astype(F32)
    onehot = jnp.where(ids[...] == slot, 1.0, 0.0).astype(BF16)
    spread[...] = lax.dot_general(onehot, flat[...], (((0,), (0,)), ((), ())), preferred_element_type=F32)
    for t in range(16):
        at = slice(8 * t, 8 * t + 8)
        vals = swap_granules([spread[at, 128 * y : 128 * y + 128] for y in range(8)])
        for x in range(8):
            grad_ref[at, 128 * x : 128 * x + 128] = vals[x]


SMEM = pl.BlockSpec(memory_space=pltpu.SMEM)
HBM = pl.BlockSpec(memory_space=pltpu.HBM)
VMEM = pl.BlockSpec(memory_space=pltpu.VMEM)


def params(mib):
    return pltpu.CompilerParams(vmem_limit_bytes=mib * MIB)


def far(array):
    return pltpu.with_memory_space_constraint(array, pltpu.HBM)


def near(array):
    return pltpu.with_memory_space_constraint(array, pltpu.VMEM)


def per_device(
    adjoint_prev, adjoint_now, speed_term, adjoint_source, forward_accel, footprint, live_counts
):
    place = jnp.stack([lax.axis_index("gx"), lax.axis_index("gy"), live_counts[0, 0, 0]]).astype(jnp.int32)
    faces_out = [pltpu.VMEM((4, CY, CZ), BF16)] * 2 + [pltpu.VMEM((CX, 4, CZ), BF16)] * 2
    level = pltpu.VMEM((1, CX, CY, CZ), F32)
    final = jax.ShapeDtypeStruct((1, CX, CY, CZ), F32)
    begun = pltpu.VMEM((OWNERS * SLABS, 4, 128), BF16)
    ext = pltpu.VMEM((CX + 8, CY, CZ), F32)
    depth = pltpu.VMEM((CX, CY, CZ), F32)

    send = pl.pallas_call(
        face_kernel,
        in_specs=[SMEM, HBM],
        out_specs=[VMEM] * 4,
        out_shape=faces_out,
        scratch_shapes=[
            pltpu.VMEM((2, 4, CY, CZ), F32), pltpu.VMEM((2, CX, 4, CZ), F32), pltpu.SemaphoreType.DMA((4,)),
        ],
        compiler_params=params(8),
        cost_estimate=pl.CostEstimate(flops=FACES_FLOPS, bytes_accessed=1_000_000, transcendentals=0),
        name="faces",
    )(place, far(adjoint_now))
    faces = swap_faces(*send)
    speed = near(speed_term)
    source = near(adjoint_source)
    forward = near(forward_accel)
    now = near(adjoint_now)
    prev = near(adjoint_prev)
    high, low, row_high, row_low = [near(jnp.asarray(term)) for term in banded(CZ, CZ) + banded(8 * CY, CY)]
    part_one = pl.pallas_call(
        first_kernel,
        in_specs=[VMEM] * 8,
        out_specs=VMEM,
        out_shape=level,
        scratch_shapes=[ext, depth],
        compiler_params=params(12),
        name="level_one",
    )(now, prev, source, speed, high, low, row_high, row_low)
    whole_one, *send = pl.pallas_call(
        first_edge_kernel,
        in_specs=[SMEM] + [VMEM] * 6,
        out_specs=[VMEM] * 5,
        out_shape=[level] + faces_out,
        input_output_aliases={1: 0},
        compiler_params=params(4),
        name="level_one_edge",
    )(place, part_one, speed, *[near(face) for face in faces[::-1]])
    faces = swap_faces(*send)
    level_one, part_two, image, outgoing, at = pl.pallas_call(
        second_kernel,
        in_specs=[SMEM] + [VMEM] * 10,
        out_specs=[HBM] + [VMEM] * 4,
        out_shape=[final, level, level, begun, jax.ShapeDtypeStruct((1, SUB), jnp.int32)],
        scratch_shapes=[ext, depth, pltpu.SemaphoreType.DMA],
        compiler_params=params(12),
        name="level_two",
    )(
        place, footprint.reshape(1, SUB), whole_one, now, speed, source, forward, high, low, row_high, row_low,
    )
    _, _, outgoing, level_two = pl.pallas_call(
        second_edge_kernel,
        in_specs=[SMEM, SMEM] + [VMEM] * 9,
        out_specs=[VMEM, VMEM, VMEM, HBM],
        out_shape=[level, level, begun, final],
        scratch_shapes=[pltpu.SemaphoreType.DMA],
        input_output_aliases={2: 0, 3: 1, 4: 2},
        compiler_params=params(4),
        name="level_two_edge",
    )(place, at, part_two, image, outgoing, speed, forward, *[near(face) for face in faces[::-1]])
    incoming = lax.all_to_all(outgoing, ("shot", "gx", "gy"), split_axis=0, concat_axis=0, tiled=True)
    gradient = pl.pallas_call(
        owner_kernel,
        in_specs=[VMEM],
        out_specs=VMEM,
        out_shape=jax.ShapeDtypeStruct((OWNERS, 1024), F32),
        scratch_shapes=[
            pltpu.VMEM((OWNERS * CAP, 128), F32),
            pltpu.VMEM((OWNERS * CAP, 1024), BF16),
            pltpu.VMEM((OWNERS, 1024), F32),
        ],
        compiler_params=params(8),
        name="owner_sum",
    )(near(incoming.reshape(OWNERS * SLABS // 2, 8, 128)))
    return (level_one, level_two, gradient)


def solution(mesh):
    return jax.shard_map(
        per_device,
        mesh=mesh,
        in_specs=(
            P("shot", "gx", "gy", None),
            P("shot", "gx", "gy", None),
            P("shot", "gx", "gy", None),
            P("shot", None, "gx", "gy", None),
            P("shot", None, "gx", "gy", None),
            P("shot", "gx", "gy", None),
            P("shot", "gx", "gy"),
        ),
        out_specs=(
            P("shot", "gx", "gy", None),
            P("shot", "gx", "gy", None),
            P(("shot", "gx", "gy"), None),
        ),
        check_vma=False,
    )
```

```python
import jax
import jax.numpy as jnp
import numpy as np
from jax import lax
from jax.experimental import pallas as pl
from jax.experimental.pallas import tpu as pltpu
from jax.sharding import PartitionSpec as P

CENTER = -205.0 / 72.0
COEFFS = (8.0 / 5.0, -1.0 / 5.0, 8.0 / 315.0, -1.0 / 560.0)

CX = 32
CY = 32
CZ = 512
OWNERS = 128
TILES_DEV = 128
CAP = 4
SUB = 512
SLABS = 9
NDEV = 8

F32 = jnp.float32
BF16 = jnp.bfloat16
FACES_FLOPS = 10_000_000_000
MIB = 1024 * 1024

SWAP_A = [(i, i ^ 1) for i in range(NDEV)]
SWAP_B = [(i, (i + 1) % NDEV if i % 2 else (i - 1) % NDEV) for i in range(NDEV)]


def banded(size, block):
    band = np.zeros((block, block), np.float64)
    for k, weight in enumerate(COEFFS, 1):
        band += weight * (np.eye(block, k=k) + np.eye(block, k=-k))
    band = np.kron(np.eye(size // block), band)
    high = band.astype(jnp.bfloat16)
    low = (band - high.astype(np.float64)).astype(jnp.bfloat16)
    return high, low


def swap_faces(x0, x1, y0, y1):
    return (
        lax.ppermute(x0, "gx", SWAP_A),
        lax.ppermute(x1, "gx", SWAP_B),
        lax.ppermute(y0, "gy", SWAP_A),
        lax.ppermute(y1, "gy", SWAP_B),
    )


def emit_faces(get_x, get_y, gx, gy, sx0, sx1, sy0, sy1):
    @pl.when(gx % 2 == 1)
    def _():
        sx0[...] = get_x(0).astype(BF16)
        sx1[...] = get_x(1).astype(BF16)

    @pl.when(gx % 2 == 0)
    def _():
        sx0[...] = get_x(1).astype(BF16)
        sx1[...] = get_x(0).astype(BF16)

    @pl.when(gy % 2 == 1)
    def _():
        sy0[...] = get_y(0).astype(BF16)
        sy1[...] = get_y(1).astype(BF16)

    @pl.when(gy % 2 == 0)
    def _():
        sy0[...] = get_y(1).astype(BF16)
        sy1[...] = get_y(0).astype(BF16)


def face_kernel(now_hbm, sx0, sx1, sy0, sy1, xs, ys, sems):
    gx = lax.axis_index("gx")
    gy = lax.axis_index("gy")
    copies = [
        pltpu.make_async_copy(now_hbm.at[0, 0:4], xs.at[0], sems.at[0]),
        pltpu.make_async_copy(now_hbm.at[0, 28:32], xs.at[1], sems.at[1]),
        pltpu.make_async_copy(now_hbm.at[0, :, 0:4, :], ys.at[0], sems.at[2]),
        pltpu.make_async_copy(now_hbm.at[0, :, 28:32, :], ys.at[1], sems.at[3]),
    ]
    for copy in copies:
        copy.start()
    for copy in copies:
        copy.wait()
    emit_faces(
        lambda side: xs[side], lambda side: ys[side], gx, gy, sx0, sx1, sy0, sy1
    )


def plane_terms(block, bands):
    high, low, row_high, row_low = bands
    block = block.reshape(8 * CY, CZ)
    big = block.astype(BF16)
    small = (block - big.astype(F32)).astype(BF16)
    term = jnp.dot(big, high[...], preferred_element_type=F32)
    term = term + jnp.dot(big, low[...], preferred_element_type=F32)
    term = term + jnp.dot(small, high[...], preferred_element_type=F32)
    term = term + jnp.dot(row_high[...], big, preferred_element_type=F32)
    term = term + jnp.dot(row_low[...], big, preferred_element_type=F32)
    term = term + jnp.dot(row_high[...], small, preferred_element_type=F32)
    return term.reshape(8, CY, CZ)


def prepare(values, ext, zs, bands):
    ext[0:4] = jnp.zeros((4, CY, CZ), F32)
    ext[36:40] = jnp.zeros((4, CY, CZ), F32)
    for i in range(4):
        block = values[0, 8 * i : 8 * i + 8]
        ext[8 * i + 4 : 8 * i + 12] = block
        zs[8 * i : 8 * i + 8] = plane_terms(block, bands)


def laplace_rows(ext, zs, x, ty):
    rows = slice(8 * ty, 8 * ty + 8)
    middle = ext[x + 4, rows, :]
    summed = (3.0 * CENTER) * middle + zs[x, rows, :]
    for k, weight in enumerate(COEFFS, 1):
        summed = summed + weight * (ext[x + 4 + k, rows, :] + ext[x + 4 - k, rows, :])
    return summed, middle


def place_pieces(foot_ref, odd, at_ref, out_ref):
    listed = foot_ref[...]
    owner = listed // TILES_DEV % OWNERS
    slot = jnp.where(listed < OWNERS * TILES_DEV, listed % TILES_DEV, -1)
    match = owner == lax.broadcasted_iota(jnp.int32, (OWNERS, SUB), 0)
    earlier = lax.broadcasted_iota(jnp.int32, (SUB, SUB), 0) < lax.broadcasted_iota(jnp.int32, (SUB, SUB), 1)
    ahead = jnp.dot(
        jnp.where(match, 1.0, 0.0).astype(BF16), jnp.where(earlier, 1.0, 0.0).astype(BF16), preferred_element_type=F32
    )
    rank = jnp.sum(jnp.where(match, ahead, 0.0), axis=0, keepdims=True).astype(jnp.int32)
    at_ref[...] = owner * SLABS + 2 * rank + odd
    order = owner * CAP + rank
    chosen = jnp.where(lax.broadcasted_iota(jnp.int32, (SUB, SUB), 0) == order, 1.0, 0.0).astype(BF16)
    slots = lax.dot_general(
        chosen, jnp.broadcast_to(slot.astype(F32), (OWNERS, SUB)).astype(BF16), (((1,), (1,)), ((), ())),
        preferred_element_type=F32,
    ).astype(BF16)
    for o in range(OWNERS):
        out_ref[o * SLABS + jnp.where(odd == 1, 0, SLABS - 1)] = slots[CAP * o : CAP * o + CAP]


def first_kernel(
    now_ref, prev_ref, source_ref, speed_ref, high, low, row_high, row_low, one_ref, ext, zs,
):
    bands = (high, low, row_high, row_low)
    prepare(now_ref, ext, zs, bands)

    def plane(x, carry):
        for ty in range(4):
            rows = slice(8 * ty, 8 * ty + 8)
            summed, middle = laplace_rows(ext, zs, x, ty)
            one_ref[0, x, rows, :] = (
                2.0 * middle - prev_ref[0, x, rows, :] + speed_ref[0, x, rows, :] * summed
                + source_ref[0, 0, x, rows, :]
            )
        return carry

    lax.fori_loop(0, CX, plane, 0)


def second_kernel(
    foot_ref, one_ref, now_ref, speed_ref, source_ref, forward_ref, high, low, row_high, row_low,
    done_hbm, two_ref, image_ref, out_ref, at_smem, ext, zs, at_ref, sem, at_sem,
):
    bands = (high, low, row_high, row_low)
    copy = pltpu.make_async_copy(one_ref, done_hbm, sem)
    copy.start()
    place_pieces(foot_ref, lax.axis_index("gy") % 2, at_ref, out_ref)
    at_copy = pltpu.make_async_copy(at_ref, at_smem, at_sem)
    at_copy.start()
    prepare(one_ref, ext, zs, bands)

    def plane(x, carry):
        for ty in range(4):
            rows = slice(8 * ty, 8 * ty + 8)
            summed, middle = laplace_rows(ext, zs, x, ty)
            two = (
                2.0 * middle - now_ref[0, x, rows, :] + speed_ref[0, x, rows, :] * summed
                + source_ref[0, 1, x, rows, :]
            )
            two_ref[0, x, rows, :] = two
            image_ref[0, x, rows, :] = forward_ref[0, 0, x, rows, :] * middle + forward_ref[0, 1, x, rows, :] * two
        return carry

    lax.fori_loop(0, CX, plane, 0)
    at_copy.wait()
    copy.wait()


def add_halos(rx0, rx1, ry0, ry1, gx, gy, update):
    def store(changes):
        for ref, at, value in changes:
            ref[at] = value

    def x_sides(low, high):
        inside = [jnp.where(gx > 0, 1.0, 0.0), jnp.where(gx < NDEV - 1, 1.0, 0.0)]

        def strip(ty, carry):
            rows = pl.ds(pl.multiple_of(8 * ty, 8), 8)
            for side, face in enumerate((low, high)):
                layers = [face[h, rows, :].astype(F32) * inside[side] for h in range(4)]
                changes = []
                for j in range(4):
                    near_first = layers[::-1] if side == 0 else layers
                    term = sum(COEFFS[j + h] * near_first[h] for h in range(4 - j))
                    changes += update(j if side == 0 else CX - 1 - j, rows, slice(0, CZ), term)
                store(changes)
            return carry

        lax.fori_loop(0, 4, strip, 0)

    def y_sides(low, high):
        inside = [jnp.where(gy > 0, 1.0, 0.0), jnp.where(gy < NDEV - 1, 1.0, 0.0)]
        row = lax.broadcasted_iota(jnp.int32, (8, 128), 0)

        def column(side, h):
            total = jnp.zeros((8, 128), F32)
            for j in range(4):
                k = 4 + j - h if side == 0 else h + 1 + j
                if k <= 4:
                    total = jnp.where(row == (j if side == 0 else 7 - j), COEFFS[k - 1] * inside[side], total)
            return total

        columns = [[column(side, h) for h in range(4)] for side in range(2)]

        def planes(i, carry):
            changes = []
            for b in range(4):
                x = 4 * i + b
                for side, face in enumerate((low, high)):
                    layers = face[x].astype(F32)
                    for zv in range(4):
                        lanes = slice(128 * zv, 128 * zv + 128)
                        term = sum(
                            columns[side][h] * jnp.broadcast_to(layers[h : h + 1, lanes], (8, 128)) for h in range(4)
                        )
                        changes += update(x, slice(24 * side, 24 * side + 8), lanes, term)
            store(changes)
            return carry

        lax.fori_loop(0, CX // 4, planes, 0)

    @pl.when(gx % 2 == 1)
    def _():
        x_sides(rx0, rx1)

    @pl.when(gx % 2 == 0)
    def _():
        x_sides(rx1, rx0)

    @pl.when(gy % 2 == 1)
    def _():
        y_sides(ry0, ry1)

    @pl.when(gy % 2 == 0)
    def _():
        y_sides(ry1, ry0)


def first_edge_kernel(part_ref, speed_ref, ry0, ry1, rx0, rx1, one_ref, sx0, sx1, sy0, sy1):
    del part_ref
    gx = lax.axis_index("gx")
    gy = lax.axis_index("gy")

    def update(x, rows, lanes, term):
        at = (0, x, rows, lanes)
        return [(one_ref, at, one_ref[at] + speed_ref[at] * term)]

    add_halos(rx0, rx1, ry0, ry1, gx, gy, update)
    emit_faces(
        lambda side: one_ref[0, 28 * side : 28 * side + 4],
        lambda side: one_ref[0, :, 28 * side : 28 * side + 4, :],
        gx, gy, sx0, sx1, sy0, sy1,
    )


def swap_granules(vals):
    granule = lax.broadcasted_iota(jnp.int32, vals[0].shape, 1) // 16
    vals = list(vals)
    for bit in (1, 2, 4):
        mask = (granule & bit) != 0
        for i in range(8):
            if i & bit:
                continue
            low, high = vals[i], vals[i + bit]
            vals[i] = jnp.where(mask, pltpu.roll(high, 16 * bit, 1), low)
            vals[i + bit] = jnp.where(mask, high, pltpu.roll(low, 128 - 16 * bit, 1))
    return vals


def second_edge_kernel(
    at_ref, part_ref, image_in, begun_ref, speed_ref, forward_ref, ry0, ry1, rx0, rx1,
    two_ref, image_ref, out_ref, done_hbm, sem,
):
    del part_ref, image_in, begun_ref
    gx = lax.axis_index("gx")
    gy = lax.axis_index("gy")

    def update(x, rows, lanes, term):
        at = (0, x, rows, lanes)
        change = speed_ref[at] * term
        return [
            (two_ref, at, two_ref[at] + change),
            (image_ref, at, image_ref[at] + forward_ref[0, 1, x, rows, lanes] * change),
        ]

    add_halos(rx0, rx1, ry0, ry1, gx, gy, update)
    copy = pltpu.make_async_copy(two_ref, done_hbm, sem)
    copy.start()

    def column(tx, carry):
        for pair in range(2):
            for zv in range(4):
                pieces = swap_granules(
                    [
                        image_ref[0, 8 * tx + x, 16 * pair : 16 * pair + 16, 128 * zv : 128 * zv + 128].astype(BF16)
                        for x in range(8)
                    ]
                )
                for p in range(8):
                    for half in range(2):
                        at = at_ref[0, tx * 128 + (2 * pair + half) * 32 + zv * 8 + p]
                        out_ref[at] = pieces[p][8 * half : 8 * half + 4]
                        out_ref[at + 1] = pieces[p][8 * half + 4 : 8 * half + 8]
        return carry

    lax.fori_loop(0, 4, column, 0)
    copy.wait()


def owner_kernel(in_ref, grad_ref, ids, flat, spread):
    def unpack(j, carry):
        lines = []
        slots = []
        for b in range(2):
            base = SLABS * (2 * j + b)
            pieces = [in_ref[base + k + k // CAP].astype(F32) for k in range(2 * CAP)]
            lines.append(jnp.swapaxes(jnp.stack(pieces), 0, 1))
            slots.append(in_ref[base + CAP].astype(F32))
        at = pl.ds(pl.multiple_of(16 * j, 16), 16)
        for y in range(8):
            flat[at, 128 * y : 128 * y + 128] = jnp.concatenate([lines[0][y], lines[1][y]], axis=0).astype(BF16)
        ids[at, :] = jnp.concatenate(slots, axis=0)
        return carry

    lax.fori_loop(0, OWNERS // 4, unpack, 0, unroll=4)
    slot = lax.broadcasted_iota(jnp.int32, (OWNERS * CAP, 128), 1).astype(F32)
    onehot = jnp.where(ids[...] == slot, 1.0, 0.0).astype(BF16)
    spread[...] = lax.dot_general(onehot, flat[...], (((0,), (0,)), ((), ())), preferred_element_type=F32)
    for t in range(16):
        at = slice(8 * t, 8 * t + 8)
        vals = swap_granules([spread[at, 128 * y : 128 * y + 128] for y in range(8)])
        for x in range(8):
            grad_ref[at, 128 * x : 128 * x + 128] = vals[x]


SMEM = pl.BlockSpec(memory_space=pltpu.SMEM)
HBM = pl.BlockSpec(memory_space=pltpu.HBM)
VMEM = pl.BlockSpec(memory_space=pltpu.VMEM)


def params(mib):
    return pltpu.CompilerParams(vmem_limit_bytes=mib * MIB)


def far(array):
    return pltpu.with_memory_space_constraint(array, pltpu.HBM)


def near(array):
    return pltpu.with_memory_space_constraint(array, pltpu.VMEM)


def per_device(
    adjoint_prev, adjoint_now, speed_term, adjoint_source, forward_accel, footprint, live_counts
):
    piece = lax.broadcasted_iota(jnp.int32, footprint.shape, 3)
    marked = jnp.where(piece < live_counts[..., None], footprint, footprint + OWNERS * TILES_DEV)
    marked = near(marked.reshape(1, SUB))
    faces_out = [pltpu.VMEM((4, CY, CZ), BF16)] * 2 + [pltpu.VMEM((CX, 4, CZ), BF16)] * 2
    level = pltpu.VMEM((1, CX, CY, CZ), F32)
    final = jax.ShapeDtypeStruct((1, CX, CY, CZ), F32)
    begun = pltpu.VMEM((OWNERS * SLABS, 4, 128), BF16)
    ext = pltpu.VMEM((CX + 8, CY, CZ), F32)
    depth = pltpu.VMEM((CX, CY, CZ), F32)

    send = pl.pallas_call(
        face_kernel,
        in_specs=[HBM],
        out_specs=[VMEM] * 4,
        out_shape=faces_out,
        scratch_shapes=[
            pltpu.VMEM((2, 4, CY, CZ), F32), pltpu.VMEM((2, CX, 4, CZ), F32), pltpu.SemaphoreType.DMA((4,)),
        ],
        compiler_params=params(8),
        cost_estimate=pl.CostEstimate(flops=FACES_FLOPS, bytes_accessed=1_000_000, transcendentals=0),
        name="faces",
    )(far(adjoint_now))
    faces = swap_faces(*send)
    speed = near(speed_term)
    source = near(adjoint_source)
    forward = near(forward_accel)
    now = near(adjoint_now)
    prev = near(adjoint_prev)
    high, low, row_high, row_low = [near(jnp.asarray(term)) for term in banded(CZ, CZ) + banded(8 * CY, CY)]
    part_one = pl.pallas_call(
        first_kernel,
        in_specs=[VMEM] * 8,
        out_specs=VMEM,
        out_shape=level,
        scratch_shapes=[ext, depth],
        compiler_params=params(12),
        name="level_one",
    )(now, prev, source, speed, high, low, row_high, row_low)
    whole_one, *send = pl.pallas_call(
        first_edge_kernel,
        in_specs=[VMEM] * 6,
        out_specs=[VMEM] * 5,
        out_shape=[level] + faces_out,
        input_output_aliases={0: 0},
        compiler_params=params(4),
        name="level_one_edge",
    )(part_one, speed, *[near(faces[i]) for i in (2, 3, 0, 1)])
    faces = swap_faces(*send)
    level_one, part_two, image, outgoing, at = pl.pallas_call(
        second_kernel,
        in_specs=[VMEM] * 10,
        out_specs=[HBM, VMEM, VMEM, VMEM, SMEM],
        out_shape=[final, level, level, begun, pltpu.SMEM((1, SUB), jnp.int32)],
        scratch_shapes=[
            ext, depth, pltpu.VMEM((1, SUB), jnp.int32), pltpu.SemaphoreType.DMA, pltpu.SemaphoreType.DMA,
        ],
        compiler_params=params(12),
        name="level_two",
    )(
        marked, whole_one, now, speed, source, forward, high, low, row_high, row_low,
    )
    _, _, outgoing, level_two = pl.pallas_call(
        second_edge_kernel,
        in_specs=[SMEM] + [VMEM] * 9,
        out_specs=[VMEM, VMEM, VMEM, HBM],
        out_shape=[level, level, begun, final],
        scratch_shapes=[pltpu.SemaphoreType.DMA],
        input_output_aliases={1: 0, 2: 1, 3: 2},
        compiler_params=params(4),
        name="level_two_edge",
    )(at, part_two, image, outgoing, speed, forward, *[near(faces[i]) for i in (2, 3, 0, 1)])
    incoming = lax.all_to_all(outgoing, ("shot", "gx", "gy"), split_axis=0, concat_axis=0, tiled=True)
    gradient = pl.pallas_call(
        owner_kernel,
        in_specs=[VMEM],
        out_specs=VMEM,
        out_shape=jax.ShapeDtypeStruct((OWNERS, 1024), F32),
        scratch_shapes=[
            pltpu.VMEM((OWNERS * CAP, 128), F32),
            pltpu.VMEM((OWNERS * CAP, 1024), BF16),
            pltpu.VMEM((OWNERS, 1024), F32),
        ],
        compiler_params=params(8),
        name="owner_sum",
    )(near(incoming.reshape(OWNERS * SLABS // 2, 8, 128)))
    return (level_one, level_two, gradient)


def solution(mesh):
    return jax.shard_map(
        per_device,
        mesh=mesh,
        in_specs=(
            P("shot", "gx", "gy", None),
            P("shot", "gx", "gy", None),
            P("shot", "gx", "gy", None),
            P("shot", None, "gx", "gy", None),
            P("shot", None, "gx", "gy", None),
            P("shot", "gx", "gy", None),
            P("shot", "gx", "gy"),
        ),
        out_specs=(
            P("shot", "gx", "gy", None),
            P("shot", "gx", "gy", None),
            P(("shot", "gx", "gy"), None),
        ),
        check_vma=False,
    )
```

```python
import jax
import jax.numpy as jnp
import numpy as np
from jax import lax
from jax.experimental import pallas as pl
from jax.experimental.pallas import tpu as pltpu
from jax.sharding import PartitionSpec as P

CENTER = -205.0 / 72.0
COEFFS = (8.0 / 5.0, -1.0 / 5.0, 8.0 / 315.0, -1.0 / 560.0)

CX = 32
CY = 32
CZ = 512
OWNERS = 128
TILES_DEV = 128
CAP = 4
SUB = 512
SLABS = 9
NDEV = 8

F32 = jnp.float32
BF16 = jnp.bfloat16
FACES_FLOPS = 10_000_000_000
MIB = 1024 * 1024

SWAP_A = [(i, i ^ 1) for i in range(NDEV)]
SWAP_B = [(i, (i + 1) % NDEV if i % 2 else (i - 1) % NDEV) for i in range(NDEV)]


def banded(size, block):
    band = np.zeros((block, block), np.float64)
    for k, weight in enumerate(COEFFS, 1):
        band += weight * (np.eye(block, k=k) + np.eye(block, k=-k))
    band = np.kron(np.eye(size // block), band)
    high = band.astype(jnp.bfloat16)
    low = (band - high.astype(np.float64)).astype(jnp.bfloat16)
    return high, low


def swap_faces(x0, x1, y0, y1):
    return (
        lax.ppermute(x0, "gx", SWAP_A),
        lax.ppermute(x1, "gx", SWAP_B),
        lax.ppermute(y0, "gy", SWAP_A),
        lax.ppermute(y1, "gy", SWAP_B),
    )


def emit_faces(get_x, get_y, gx, gy, sx0, sx1, sy0, sy1):
    @pl.when(gx % 2 == 1)
    def _():
        sx0[...] = get_x(0).astype(BF16)
        sx1[...] = get_x(1).astype(BF16)

    @pl.when(gx % 2 == 0)
    def _():
        sx0[...] = get_x(1).astype(BF16)
        sx1[...] = get_x(0).astype(BF16)

    @pl.when(gy % 2 == 1)
    def _():
        sy0[...] = get_y(0).astype(BF16)
        sy1[...] = get_y(1).astype(BF16)

    @pl.when(gy % 2 == 0)
    def _():
        sy0[...] = get_y(1).astype(BF16)
        sy1[...] = get_y(0).astype(BF16)


def face_kernel(now_hbm, sx0, sx1, sy0, sy1, xs, ys, sems):
    gx = lax.axis_index("gx")
    gy = lax.axis_index("gy")
    copies = [
        pltpu.make_async_copy(now_hbm.at[0, 0:4], xs.at[0], sems.at[0]),
        pltpu.make_async_copy(now_hbm.at[0, 28:32], xs.at[1], sems.at[1]),
        pltpu.make_async_copy(now_hbm.at[0, :, 0:4, :], ys.at[0], sems.at[2]),
        pltpu.make_async_copy(now_hbm.at[0, :, 28:32, :], ys.at[1], sems.at[3]),
    ]
    for copy in copies:
        copy.start()
    for copy in copies:
        copy.wait()
    emit_faces(
        lambda side: xs[side], lambda side: ys[side], gx, gy, sx0, sx1, sy0, sy1
    )


def plane_terms(block, bands):
    high, low, row_high, row_low = bands
    block = block.reshape(8 * CY, CZ)
    big = block.astype(BF16)
    small = (block - big.astype(F32)).astype(BF16)
    term = jnp.dot(big, high[...], preferred_element_type=F32)
    term = term + jnp.dot(big, low[...], preferred_element_type=F32)
    term = term + jnp.dot(small, high[...], preferred_element_type=F32)
    term = term + jnp.dot(row_high[...], big, preferred_element_type=F32)
    term = term + jnp.dot(row_low[...], big, preferred_element_type=F32)
    term = term + jnp.dot(row_high[...], small, preferred_element_type=F32)
    return term.reshape(8, CY, CZ)


def prepare(values, ext, zs, bands):
    ext[0:4] = jnp.zeros((4, CY, CZ), F32)
    ext[36:40] = jnp.zeros((4, CY, CZ), F32)
    for i in range(4):
        block = values[0, 8 * i : 8 * i + 8]
        ext[8 * i + 4 : 8 * i + 12] = block
        zs[8 * i : 8 * i + 8] = plane_terms(block, bands)


def laplace_rows(ext, zs, x, ty):
    rows = slice(8 * ty, 8 * ty + 8)
    middle = ext[x + 4, rows, :]
    summed = (3.0 * CENTER) * middle + zs[x, rows, :]
    for k, weight in enumerate(COEFFS, 1):
        summed = summed + weight * (ext[x + 4 + k, rows, :] + ext[x + 4 - k, rows, :])
    return summed, middle


def place_pieces(foot_ref, odd, at_ref, out_ref):
    listed = foot_ref[...]
    owner = listed // TILES_DEV % OWNERS
    slot = jnp.where(listed < OWNERS * TILES_DEV, listed % TILES_DEV, -1)
    match = owner == lax.broadcasted_iota(jnp.int32, (OWNERS, SUB), 0)
    earlier = lax.broadcasted_iota(jnp.int32, (SUB, SUB), 0) < lax.broadcasted_iota(jnp.int32, (SUB, SUB), 1)
    ahead = jnp.dot(
        jnp.where(match, 1.0, 0.0).astype(BF16), jnp.where(earlier, 1.0, 0.0).astype(BF16), preferred_element_type=F32
    )
    rank = jnp.sum(jnp.where(match, ahead, 0.0), axis=0, keepdims=True).astype(jnp.int32)
    at_ref[...] = owner * SLABS + 2 * rank + odd
    order = owner * CAP + rank
    chosen = jnp.where(lax.broadcasted_iota(jnp.int32, (SUB, SUB), 0) == order, 1.0, 0.0).astype(BF16)
    slots = lax.dot_general(
        chosen, jnp.broadcast_to(slot.astype(F32), (OWNERS, SUB)).astype(BF16), (((1,), (1,)), ((), ())),
        preferred_element_type=F32,
    ).astype(BF16)
    for o in range(OWNERS):
        out_ref[o * SLABS + jnp.where(odd == 1, 0, SLABS - 1)] = slots[CAP * o : CAP * o + CAP]


def first_kernel(
    now_ref, prev_ref, source_ref, speed_ref, high, low, row_high, row_low, one_ref, ext, zs,
):
    bands = (high, low, row_high, row_low)
    prepare(now_ref, ext, zs, bands)

    def plane(x, carry):
        for ty in range(4):
            rows = slice(8 * ty, 8 * ty + 8)
            summed, middle = laplace_rows(ext, zs, x, ty)
            one_ref[0, x, rows, :] = (
                2.0 * middle - prev_ref[0, x, rows, :] + speed_ref[0, x, rows, :] * summed
                + source_ref[0, 0, x, rows, :]
            )
        return carry

    lax.fori_loop(0, CX, plane, 0)


def second_kernel(
    foot_ref, one_ref, now_ref, speed_ref, source_ref, forward_ref, high, low, row_high, row_low,
    done_hbm, two_ref, image_ref, out_ref, at_smem, ext, zs, at_ref, sem, at_sem,
):
    bands = (high, low, row_high, row_low)
    copy = pltpu.make_async_copy(one_ref, done_hbm, sem)
    copy.start()
    place_pieces(foot_ref, lax.axis_index("gy") % 2, at_ref, out_ref)
    at_copy = pltpu.make_async_copy(at_ref, at_smem, at_sem)
    at_copy.start()
    prepare(one_ref, ext, zs, bands)

    def plane(x, carry):
        for ty in range(4):
            rows = slice(8 * ty, 8 * ty + 8)
            summed, middle = laplace_rows(ext, zs, x, ty)
            two = (
                2.0 * middle - now_ref[0, x, rows, :] + speed_ref[0, x, rows, :] * summed
                + source_ref[0, 1, x, rows, :]
            )
            two_ref[0, x, rows, :] = two
            image_ref[0, x, rows, :] = forward_ref[0, 0, x, rows, :] * middle + forward_ref[0, 1, x, rows, :] * two
        return carry

    lax.fori_loop(0, CX, plane, 0)
    at_copy.wait()
    copy.wait()


def add_halos(rx0, rx1, ry0, ry1, gx, gy, update):
    def store(changes):
        for ref, at, value in changes:
            ref[at] = value

    def x_sides(low, high):
        inside = [jnp.where(gx > 0, 1.0, 0.0), jnp.where(gx < NDEV - 1, 1.0, 0.0)]

        def strip(ty, carry):
            rows = pl.ds(pl.multiple_of(8 * ty, 8), 8)
            for side, face in enumerate((low, high)):
                layers = [face[h, rows, :].astype(F32) * inside[side] for h in range(4)]
                changes = []
                for j in range(4):
                    near_first = layers[::-1] if side == 0 else layers
                    term = sum(COEFFS[j + h] * near_first[h] for h in range(4 - j))
                    changes += update(j if side == 0 else CX - 1 - j, rows, slice(0, CZ), term)
                store(changes)
            return carry

        lax.fori_loop(0, 4, strip, 0)

    def y_sides(low, high):
        inside = [jnp.where(gy > 0, 1.0, 0.0), jnp.where(gy < NDEV - 1, 1.0, 0.0)]
        row = lax.broadcasted_iota(jnp.int32, (8, 128), 0)

        def column(side, h):
            total = jnp.zeros((8, 128), F32)
            for j in range(4):
                k = 4 + j - h if side == 0 else h + 1 + j
                if k <= 4:
                    total = jnp.where(row == (j if side == 0 else 7 - j), COEFFS[k - 1] * inside[side], total)
            return total

        columns = [[column(side, h) for h in range(4)] for side in range(2)]

        def planes(i, carry):
            changes = []
            for b in range(4):
                x = 4 * i + b
                for side, face in enumerate((low, high)):
                    layers = face[x].astype(F32)
                    for zv in range(4):
                        lanes = slice(128 * zv, 128 * zv + 128)
                        term = sum(
                            columns[side][h] * jnp.broadcast_to(layers[h : h + 1, lanes], (8, 128)) for h in range(4)
                        )
                        changes += update(x, slice(24 * side, 24 * side + 8), lanes, term)
            store(changes)
            return carry

        lax.fori_loop(0, CX // 4, planes, 0)

    @pl.when(gx % 2 == 1)
    def _():
        x_sides(rx0, rx1)

    @pl.when(gx % 2 == 0)
    def _():
        x_sides(rx1, rx0)

    @pl.when(gy % 2 == 1)
    def _():
        y_sides(ry0, ry1)

    @pl.when(gy % 2 == 0)
    def _():
        y_sides(ry1, ry0)


def first_edge_kernel(part_ref, speed_ref, ry0, ry1, rx1, rx0, one_ref, sx0, sx1, sy0, sy1):
    del part_ref
    gx = lax.axis_index("gx")
    gy = lax.axis_index("gy")

    def update(x, rows, lanes, term):
        at = (0, x, rows, lanes)
        return [(one_ref, at, one_ref[at] + speed_ref[at] * term)]

    add_halos(rx0, rx1, ry0, ry1, gx, gy, update)
    emit_faces(
        lambda side: one_ref[0, 28 * side : 28 * side + 4],
        lambda side: one_ref[0, :, 28 * side : 28 * side + 4, :],
        gx, gy, sx0, sx1, sy0, sy1,
    )


def swap_granules(vals):
    granule = lax.broadcasted_iota(jnp.int32, vals[0].shape, 1) // 16
    vals = list(vals)
    for bit in (1, 2, 4):
        mask = (granule & bit) != 0
        for i in range(8):
            if i & bit:
                continue
            low, high = vals[i], vals[i + bit]
            vals[i] = jnp.where(mask, pltpu.roll(high, 16 * bit, 1), low)
            vals[i + bit] = jnp.where(mask, high, pltpu.roll(low, 128 - 16 * bit, 1))
    return vals


def second_edge_kernel(
    at_ref, part_ref, image_in, begun_ref, speed_ref, forward_ref, ry0, ry1, rx1, rx0,
    two_ref, image_ref, out_ref, done_hbm, sem,
):
    del part_ref, image_in, begun_ref
    gx = lax.axis_index("gx")
    gy = lax.axis_index("gy")

    def update(x, rows, lanes, term):
        at = (0, x, rows, lanes)
        change = speed_ref[at] * term
        return [
            (two_ref, at, two_ref[at] + change),
            (image_ref, at, image_ref[at] + forward_ref[0, 1, x, rows, lanes] * change),
        ]

    add_halos(rx0, rx1, ry0, ry1, gx, gy, update)
    copy = pltpu.make_async_copy(two_ref, done_hbm, sem)
    copy.start()

    def column(tx, carry):
        for pair in range(2):
            for zv in range(4):
                pieces = swap_granules(
                    [
                        image_ref[0, 8 * tx + x, 16 * pair : 16 * pair + 16, 128 * zv : 128 * zv + 128].astype(BF16)
                        for x in range(8)
                    ]
                )
                for p in range(8):
                    for half in range(2):
                        at = at_ref[0, tx * 128 + (2 * pair + half) * 32 + zv * 8 + p]
                        out_ref[at] = pieces[p][8 * half : 8 * half + 4]
                        out_ref[at + 1] = pieces[p][8 * half + 4 : 8 * half + 8]
        return carry

    lax.fori_loop(0, 4, column, 0)
    copy.wait()


def owner_kernel(in_ref, grad_ref, ids, flat, spread):
    def unpack(j, carry):
        lines = []
        slots = []
        for b in range(2):
            base = SLABS * (2 * j + b)
            pieces = [in_ref[base + k + k // CAP].astype(F32) for k in range(2 * CAP)]
            lines.append(jnp.swapaxes(jnp.stack(pieces), 0, 1))
            slots.append(in_ref[base + CAP].astype(F32))
        at = pl.ds(pl.multiple_of(16 * j, 16), 16)
        for y in range(8):
            flat[at, 128 * y : 128 * y + 128] = jnp.concatenate([lines[0][y], lines[1][y]], axis=0).astype(BF16)
        ids[at, :] = jnp.concatenate(slots, axis=0)
        return carry

    lax.fori_loop(0, OWNERS // 4, unpack, 0, unroll=4)
    slot = lax.broadcasted_iota(jnp.int32, (OWNERS * CAP, 128), 1).astype(F32)
    onehot = jnp.where(ids[...] == slot, 1.0, 0.0).astype(BF16)
    spread[...] = lax.dot_general(onehot, flat[...], (((0,), (0,)), ((), ())), preferred_element_type=F32)
    for t in range(16):
        at = slice(8 * t, 8 * t + 8)
        vals = swap_granules([spread[at, 128 * y : 128 * y + 128] for y in range(8)])
        for x in range(8):
            grad_ref[at, 128 * x : 128 * x + 128] = vals[x]


SMEM = pl.BlockSpec(memory_space=pltpu.SMEM)
HBM = pl.BlockSpec(memory_space=pltpu.HBM)
VMEM = pl.BlockSpec(memory_space=pltpu.VMEM)


def params(mib):
    return pltpu.CompilerParams(vmem_limit_bytes=mib * MIB)


def far(array):
    return pltpu.with_memory_space_constraint(array, pltpu.HBM)


def near(array):
    return pltpu.with_memory_space_constraint(array, pltpu.VMEM)


def per_device(
    adjoint_prev, adjoint_now, speed_term, adjoint_source, forward_accel, footprint, live_counts
):
    piece = lax.broadcasted_iota(jnp.int32, footprint.shape, 3)
    marked = jnp.where(piece < live_counts[..., None], footprint, footprint + OWNERS * TILES_DEV)
    marked = near(marked.reshape(1, SUB))
    faces_out = [pltpu.VMEM((4, CY, CZ), BF16)] * 2 + [pltpu.VMEM((CX, 4, CZ), BF16)] * 2
    level = pltpu.VMEM((1, CX, CY, CZ), F32)
    final = jax.ShapeDtypeStruct((1, CX, CY, CZ), F32)
    begun = pltpu.VMEM((OWNERS * SLABS, 4, 128), BF16)
    ext = pltpu.VMEM((CX + 8, CY, CZ), F32)
    depth = pltpu.VMEM((CX, CY, CZ), F32)

    send = pl.pallas_call(
        face_kernel,
        in_specs=[HBM],
        out_specs=[VMEM] * 4,
        out_shape=faces_out,
        scratch_shapes=[
            pltpu.VMEM((2, 4, CY, CZ), F32), pltpu.VMEM((2, CX, 4, CZ), F32), pltpu.SemaphoreType.DMA((4,)),
        ],
        compiler_params=params(8),
        cost_estimate=pl.CostEstimate(flops=FACES_FLOPS, bytes_accessed=1_000_000, transcendentals=0),
        name="faces",
    )(far(adjoint_now))
    faces = swap_faces(*send)
    speed = near(speed_term)
    source = near(adjoint_source)
    forward = near(forward_accel)
    now = near(adjoint_now)
    prev = near(adjoint_prev)
    high, low, row_high, row_low = [near(jnp.asarray(term)) for term in banded(CZ, CZ) + banded(8 * CY, CY)]
    part_one = pl.pallas_call(
        first_kernel,
        in_specs=[VMEM] * 8,
        out_specs=VMEM,
        out_shape=level,
        scratch_shapes=[ext, depth],
        compiler_params=params(12),
        name="level_one",
    )(now, prev, source, speed, high, low, row_high, row_low)
    whole_one, *send = pl.pallas_call(
        first_edge_kernel,
        in_specs=[VMEM] * 6,
        out_specs=[VMEM] * 5,
        out_shape=[level] + faces_out,
        input_output_aliases={0: 0},
        compiler_params=params(4),
        name="level_one_edge",
    )(part_one, speed, *[near(faces[i]) for i in (2, 3, 1, 0)])
    faces = swap_faces(*send)
    level_one, part_two, image, outgoing, at = pl.pallas_call(
        second_kernel,
        in_specs=[VMEM] * 10,
        out_specs=[HBM, VMEM, VMEM, VMEM, SMEM],
        out_shape=[final, level, level, begun, pltpu.SMEM((1, SUB), jnp.int32)],
        scratch_shapes=[
            ext, depth, pltpu.VMEM((1, SUB), jnp.int32), pltpu.SemaphoreType.DMA, pltpu.SemaphoreType.DMA,
        ],
        compiler_params=params(12),
        name="level_two",
    )(
        marked, whole_one, now, speed, source, forward, high, low, row_high, row_low,
    )
    _, _, outgoing, level_two = pl.pallas_call(
        second_edge_kernel,
        in_specs=[SMEM] + [VMEM] * 9,
        out_specs=[VMEM, VMEM, VMEM, HBM],
        out_shape=[level, level, begun, final],
        scratch_shapes=[pltpu.SemaphoreType.DMA],
        input_output_aliases={1: 0, 2: 1, 3: 2},
        compiler_params=params(4),
        name="level_two_edge",
    )(at, part_two, image, outgoing, speed, forward, *[near(faces[i]) for i in (2, 3, 1, 0)])
    incoming = lax.all_to_all(outgoing, ("shot", "gx", "gy"), split_axis=0, concat_axis=0, tiled=True)
    gradient = pl.pallas_call(
        owner_kernel,
        in_specs=[VMEM],
        out_specs=VMEM,
        out_shape=jax.ShapeDtypeStruct((OWNERS, 1024), F32),
        scratch_shapes=[
            pltpu.VMEM((OWNERS * CAP, 128), F32),
            pltpu.VMEM((OWNERS * CAP, 1024), BF16),
            pltpu.VMEM((OWNERS, 1024), F32),
        ],
        compiler_params=params(8),
        name="owner_sum",
    )(near(incoming.reshape(OWNERS * SLABS // 2, 8, 128)))
    return (level_one, level_two, gradient)


def solution(mesh):
    return jax.shard_map(
        per_device,
        mesh=mesh,
        in_specs=(
            P("shot", "gx", "gy", None),
            P("shot", "gx", "gy", None),
            P("shot", "gx", "gy", None),
            P("shot", None, "gx", "gy", None),
            P("shot", None, "gx", "gy", None),
            P("shot", "gx", "gy", None),
            P("shot", "gx", "gy"),
        ),
        out_specs=(
            P("shot", "gx", "gy", None),
            P("shot", "gx", "gy", None),
            P(("shot", "gx", "gy"), None),
        ),
        check_vma=False,
    )
```
